32 devices in a mesh: cuts: 2 (over x), gz: 16 (over z, y, core).
Axes of the slice: x: 2, y: 2, z: 4, core: 2. Of those that a mesh axis runs over, the one named last changes fastest.
Arguments:
- states: float32 [2, 64, 32, 256], P('cuts', 'gz'), may hold values from -8 to 8
- conduct: float32 [64, 32, 256], P('gz'), may hold values from 0.5 to 4
Outputs:
- end_states: float32 [2, 64, 32, 256], P('cuts', 'gz')
The draws below stay inside these ranges and needn't reach their ends.
All inputs are finite; a program needn't handle non-finite values.
Results may differ from the reference program's by a relative error of at most 0.0001.
Values sent between devices are 32-bit elements; how exact they have to be, the bound alone decides.
A program may use at most 64 MiB of HBM per device.

```python
import math
import jax
import jax.numpy as jnp
from jax import lax

NX = 32
NY = 256
STEPS = 2
SWEEPS = 3
SWEEPS_C = 2
SLICES = 2
NZ = 64


def draw_states(key, part):
    base = jax.random.normal(key, (SLICES, NZ, NX, NY), jnp.float32)
    return jnp.clip(base, -8.0, 8.0)


def level_of(own_key, extent, cuts, smallest, high):
    loudness = 1.0
    for axis_at, shards_of in cuts:
        draws = jax.random.uniform(jax.random.fold_in(jax.random.fold_in(own_key, 6), axis_at), (shards_of,), jnp.float32, smallest / len(cuts), high / len(cuts))
        loudness = loudness * jnp.repeat(jnp.exp(draws), extent[axis_at] // shards_of).reshape((-1,) + (1,) * (len(extent) - 1 - axis_at))
    return loudness


def setup_inputs(seed: int = 0) -> dict:
    arg_keys = jax.random.split(jax.random.key(seed), 3)
    states = draw_states(jax.random.fold_in(arg_keys[2], 71), 0)
    conduct = jnp.clip(jnp.exp(math.log(4.0) - 2.0794415 * jax.random.uniform(arg_keys[1], (NZ, NX, NY), jnp.float32) ** level_of(arg_keys[1], (NZ, NX, NY), ((0, 16),), -0.2, 0.2)), 0.5, 4.0)
    return {"states": states, "conduct": conduct}


COUPLING = 1.0
SPREAD = 0.85


def chebyshev_weights(count):
    return [1.0 / (1.0 + SPREAD * math.cos(math.pi * (2 * index_now + 1) / (2 * count))) for index_now in range(count)]


def face_terms(conduct):
    padded = jnp.pad(conduct, 1)
    center = conduct
    lower_z = 0.5 * (center + padded[:-2, 1:-1, 1:-1])
    upper_z = 0.5 * (center + padded[2:, 1:-1, 1:-1])
    lower_x = 0.5 * (center + padded[1:-1, :-2, 1:-1])
    upper_x = 0.5 * (center + padded[1:-1, 2:, 1:-1])
    lower_y = 0.5 * (center + padded[1:-1, 1:-1, :-2])
    upper_y = 0.5 * (center + padded[1:-1, 1:-1, 2:])
    return (lower_z, upper_z, lower_x, upper_x, lower_y, upper_y)


def diagonal_of(faces, coupling):
    return 1.0 + coupling * (faces[0] + faces[1] + faces[2] + faces[3] + faces[4] + faces[5])


def operate(iterate, faces, diagonal, coupling):
    padded = jnp.pad(iterate, 1)
    beside_all = (faces[0] * padded[:-2, 1:-1, 1:-1] + faces[1] * padded[2:, 1:-1, 1:-1]
              + faces[2] * padded[1:-1, :-2, 1:-1] + faces[3] * padded[1:-1, 2:, 1:-1]
              + faces[4] * padded[1:-1, 1:-1, :-2] + faces[5] * padded[1:-1, 1:-1, 2:])
    return diagonal * iterate - coupling * beside_all


def implicit_solve(source, faces, diagonal, coupling, weights):
    iterate = source
    for weight in weights:
        iterate = iterate + weight * (source - operate(iterate, faces, diagonal, coupling)) / diagonal
    return iterate


def restrict(field):
    shaped = field.reshape(field.shape[0] // 2, 2, field.shape[1] // 2, 2, field.shape[2] // 2, 2)
    return shaped.mean(axis=(1, 3, 5))


def prolong(coarse):
    return jnp.repeat(jnp.repeat(jnp.repeat(coarse, 2, axis=0), 2, axis=1), 2, axis=2)


def reference(states, conduct):
    fine_faces = face_terms(conduct)
    fine_diag = diagonal_of(fine_faces, COUPLING)
    coarse_faces = face_terms(restrict(conduct))
    coarse_diag = diagonal_of(coarse_faces, 0.5 * COUPLING)
    fine_weights = chebyshev_weights(SWEEPS)
    coarse_weights = chebyshev_weights(SWEEPS_C)

    def propagate_fine(start):
        current = start
        for step_index in range(STEPS):
            current = implicit_solve(current, fine_faces, fine_diag, COUPLING, fine_weights)
        return current

    fine_end = lax.map(propagate_fine, states)
    carried = jnp.zeros_like(restrict(states[0]))
    outputs = []
    for index_now in range(SLICES):
        stepped = implicit_solve(carried, coarse_faces, coarse_diag, 0.5 * COUPLING, coarse_weights)
        outputs.append(fine_end[index_now] + prolong(stepped))
        if index_now + 1 < SLICES:
            carried = stepped + (restrict(fine_end[index_now]) - restrict(states[index_now + 1]))
    return jnp.stack(outputs)
```

```python
import functools
import math

import jax
import jax.numpy as jnp
from jax import lax
from jax.experimental import pallas as pl
from jax.experimental.pallas import tpu as pltpu
from jax.sharding import PartitionSpec as P

STEPS = 2
SWEEPS = 3
SWEEPS_C = 2

COUPLING = 1.0
SPREAD = 0.85
MESH = pl.DeviceIdType.MESH

HALO = 4
HALO_C = HALO // 2
ROUNDS = STEPS * SWEEPS
DEEP = ROUNDS // 2


def chebyshev_weights(count):
    return [
        1.0 / (1.0 + SPREAD * math.cos(math.pi * (2 * index_now + 1) / (2 * count)))
        for index_now in range(count)
    ]


def down(v, axis):
    return pltpu.roll(v, 1, axis)


def up(v, axis):
    return pltpu.roll(v, v.shape[axis] - 1, axis)


def coefficient_layer(k_ref, bx, by, inv, l, coupling, keep):
    shape = k_ref.shape[1:]
    at_x = lax.broadcasted_iota(jnp.int32, shape, 0)
    at_y = lax.broadcasted_iota(jnp.int32, shape, 1)
    half = 0.5 * coupling
    k = k_ref[l]
    x_lo = jnp.where(at_x == 0, 0.0, down(k, 0))
    x_hi = jnp.where(at_x == shape[0] - 1, 0.0, up(k, 0))
    y_lo = jnp.where(at_y == 0, 0.0, down(k, 1))
    y_hi = jnp.where(at_y == shape[1] - 1, 0.0, up(k, 1))
    bx[l] = jnp.where(at_x == 0, 0.0, half * (k + x_lo))
    by[l] = jnp.where(at_y == 0, 0.0, half * (k + y_lo))
    diag = 1.0 + half * (
        6.0 * k + (x_lo + x_hi) + (y_lo + y_hi) + (k_ref[l - 1] + k_ref[l + 1])
    )
    inv[l] = keep / diag


def sweep_layer(src, source, dst, bx, by, bz, inv, l, weight):
    w = src[l]
    b_y = by[l]
    b_x = bx[l]
    total = (
        source[l]
        + (b_y * down(w, 1) + up(b_y * w, 1))
        + (b_x * down(w, 0) + up(b_x * w, 0))
        + (bz[l] * src[l - 1] + bz[l + 1] * src[l + 1])
    )
    dst[l] = (1.0 - weight) * w + (weight * inv[l]) * total


def times_exact(value, matrix):
    high = value.astype(jnp.bfloat16)
    rest = value - high.astype(jnp.float32)
    middle = rest.astype(jnp.bfloat16)
    low = (rest - middle.astype(jnp.float32)).astype(jnp.bfloat16)
    count = value.shape[0]
    parts = lax.dot_general(
        jnp.concatenate([high, middle, low], axis=0),
        matrix.astype(jnp.bfloat16),
        (((1,), (0,)), ((), ())),
        preferred_element_type=jnp.float32,
    )
    return parts[:count] + (parts[count : 2 * count] + parts[2 * count :])


def restricted(field, firsts, tmp, matrix):
    rows = tmp.shape[1]
    sums = [field[first] + field[first + 1] for first in firsts]
    narrow = times_exact(jnp.concatenate(sums, axis=0), matrix)
    out = []
    for j in range(len(sums)):
        tmp[j] = narrow[j * rows : (j + 1) * rows]
        out.append(tmp[j, pl.ds(0, rows // 2, 2), :] + tmp[j, pl.ds(1, rows // 2, 2), :])
    return out


def kernel(
    cut_count, gz_count, layers,
    s_in, k_in, out,
    k, w0, w1, w2, w3, w4, w5, w6, bx, by, bz, inv, tmp,
    kc, cx, cy, cz, cinv, rs, car, ca, cb, car_own, car_out, car_in, outgoing,
    load_sem, send_sem, recv_sem,
):
    cut = lax.axis_index("cuts")
    gz = lax.axis_index("gz")
    side = lax.rem(gz, 2)
    outer, inner = gz - 1 + 2 * side, gz + 1 - 2 * side
    has_outer = jnp.logical_and(outer >= 0, outer < gz_count)
    has_prev, has_next = cut > 0, cut < cut_count - 1
    odd = lax.rem(cut, 2) == 1
    relayed = jnp.logical_and(jnp.logical_not(odd), has_next)
    coarse = layers // 2
    always = None
    w = (w0, w1, w2, w3, w4, w5, w6)

    def at(u):
        return HALO + u

    def place(u):
        return u + side * (layers - 1 - 2 * u)

    def when(condition, act):
        if condition is always:
            act()
        else:
            pl.when(condition)(act)

    loads_k = [
        pltpu.make_async_copy(k_in.at[place(u)], k.at[at(u)], load_sem.at[u])
        for u in range(layers)
    ]
    loads_s = [
        pltpu.make_async_copy(s_in.at[0, place(u)], w0.at[at(u)], load_sem.at[layers + u])
        for u in range(layers)
    ]
    for load in loads_k + loads_s:
        load.start()

    barrier = pltpu.get_barrier_semaphore()
    for there, ok in (
        ((cut, outer), has_outer),
        ((cut, inner), always),
        ((cut - 1, gz), has_prev),
        ((cut + 1, gz), has_next),
    ):
        when(
            ok,
            lambda there=there: pl.semaphore_signal(
                barrier, inc=1, device_id=there, device_id_type=MESH
            ),
        )
    expected = 1 + sum(ok.astype(jnp.int32) for ok in (has_outer, has_prev, has_next))

    @pl.when(jnp.logical_not(has_outer))
    def _():
        fine = jnp.zeros((HALO,) + w0.shape[1:], jnp.float32)
        for ref in (w0, k):
            ref[pl.ds(0, HALO)] = fine
        for ref in (w1, w2):
            ref[0] = fine[0]
        car_out[...] = jnp.zeros(car_out.shape, jnp.float32)

    count = [0]
    sent = []

    def remote(src, dst, there, ok, slot=None):
        index = count[0]
        count[0] += 1
        copy = pltpu.make_async_remote_copy(
            src_ref=src,
            dst_ref=dst,
            send_sem=send_sem.at[index],
            recv_sem=recv_sem.at[index if slot is None else slot],
            device_id=there,
            device_id_type=MESH,
        )
        sent.append((ok, copy))
        return copy

    to_outer, to_inner = (cut, outer), (cut, inner)
    carries = jnp.logical_and(has_outer, jnp.logical_not(relayed))
    relays = jnp.logical_and(has_outer, odd)

    def mirrored(ref, u, there, ok):
        return remote(ref.at[at(u)], ref.at[at(-1 - u)], there, ok)

    out_k = [mirrored(k, u, to_outer, carries) for u in range(HALO)]
    out_w0 = [mirrored(w0, u, to_outer, has_outer) for u in range(HALO)]
    out_w = {
        j: mirrored(w[j], HALO - 1, to_outer, has_outer) for j in range(1, DEEP)
    }
    relay_k = [
        remote(k.at[at(-1 - u)], k.at[at(-1 - u)], (cut - 1, gz), relays, slot=u)
        for u in range(HALO)
    ]

    def across(ref, i):
        return remote(ref.at[at(layers - 1 - i)], ref.at[at(layers + i)], to_inner, always)

    in_k = [across(k, i) for i in range(HALO)]
    in_w0 = [across(w0, i) for i in range(HALO)]
    in_half = [across(w[SWEEPS], i) for i in range(SWEEPS)]
    next_own = remote(outgoing, car_own, (cut + 1, gz), has_next)
    next_out = remote(
        outgoing.at[pl.ds(0, HALO_C)], car_out, (cut + 1, outer),
        jnp.logical_and(has_next, has_outer),
    )
    next_in = remote(
        outgoing.at[pl.ds(coarse - HALO_C, HALO_C)], car_in, (cut + 1, inner), has_next
    )

    keep_outer = jnp.where(has_outer, 1.0, 0.0)
    weights = chebyshev_weights(SWEEPS)
    coarse_weights = chebyshev_weights(SWEEPS_C)

    needed = []
    for j in range(1, ROUNDS + 1):
        low = -min(DEEP, ROUNDS - j)
        high = layers + (-j % SWEEPS)
        needed += [(j, u) for u in range(low, high)]
    waiting = dict.fromkeys(needed)
    have, have_k, faces, cells = set(), set(), set(), set()
    starts = {}
    for j, copy in out_w.items():
        starts[(j, HALO - 1)] = (has_outer, copy)
    for i, copy in enumerate(in_half):
        starts[(SWEEPS, layers - 1 - i)] = (always, copy)

    def coefficients(u):
        for face in (u, u + 1):
            if face not in faces:
                bz[at(face)] = 0.5 * COUPLING * (k[at(face)] + k[at(face - 1)])
                faces.add(face)
        if u not in cells:
            coefficient_layer(k, bx, by, inv, at(u), COUPLING, keep_outer if u < 0 else 1.0)
            cells.add(u)

    def advance(values=(), conductivity=()):
        have.update(values)
        have_k.update(conductivity)
        for u in range(-DEEP, layers + SWEEPS - 1):
            if u not in cells and have_k >= {u - 1, u, u + 1}:
                coefficients(u)
        moved = True
        while moved:
            moved = False
            for j, u in list(waiting):
                first = SWEEPS * ((j - 1) // SWEEPS)
                inputs = {(j - 1, u - 1), (j - 1, u), (j - 1, u + 1), (first, u)}
                if u not in cells or not have >= inputs:
                    continue
                sweep_layer(
                    w[j - 1], w[first], w[j], bx, by, bz, inv, at(u),
                    weights[(j - 1) % SWEEPS],
                )
                have.add((j, u))
                del waiting[(j, u)]
                moved = True
                if (j, u) in starts:
                    ok, copy = starts[(j, u)]
                    when(ok, copy.start)

    for load in loads_k + loads_s:
        load.wait()
    pl.semaphore_wait(barrier, expected)

    for copy in out_k:
        when(carries, copy.start)
    for copy in out_w0:
        when(has_outer, copy.start)
    for a, b in zip(in_k, in_w0):
        a.start()
        b.start()

    advance([(0, u) for u in range(layers)], range(layers))
    for i in range(HALO):
        in_k[i].wait_recv()
        in_w0[i].wait_recv()
        advance([(0, layers + i)], [layers + i])

    fine_y = w0.shape[2]
    row = lax.broadcasted_iota(jnp.int32, (fine_y, fine_y // 2), 0)
    col = lax.broadcasted_iota(jnp.int32, (fine_y, fine_y // 2), 1)
    gather = jnp.where((row == 2 * col) | (row == 2 * col + 1), 0.125, 0.0)
    every_c = range(-HALO_C, coarse + HALO_C)

    @pl.when(has_prev)
    def _():
        for u in range(HALO):
            when(has_outer, out_k[u].wait_recv)
            when(relays, relay_k[u].start)
        for c, value in zip(every_c, restricted(k, [at(2 * c) for c in every_c], tmp, gather)):
            kc[HALO_C + c] = value
        for c in range(-1, coarse + 2):
            cz[HALO_C + c] = 0.25 * COUPLING * (kc[HALO_C + c] + kc[HALO_C + c - 1])
        for c in range(-1, coarse + 1):
            coefficient_layer(
                kc, cx, cy, cinv, HALO_C + c, 0.5 * COUPLING, keep_outer if c < 0 else 1.0
            )

    first_waits = jnp.logical_and(has_outer, jnp.logical_not(has_prev))
    for u in range(HALO):
        when(first_waits, out_k[u].wait_recv)
        when(has_outer, out_w0[u].wait_recv)
        advance([(0, -1 - u)], [-1 - u])

    @pl.when(has_prev)
    def _():
        for c, value in zip(every_c, restricted(w0, [at(2 * c) for c in every_c], tmp, gather)):
            rs[HALO_C + c] = value

    for i in range(SWEEPS):
        in_half[i].wait_recv()
    advance([(SWEEPS, layers + i) for i in range(SWEEPS)])
    for j in range(1, DEEP):
        when(has_outer, out_w[j].wait_recv)
        advance([(j, -HALO)])

    @pl.when(has_next)
    def _():
        for c, value in enumerate(
            restricted(w6, [at(2 * c) for c in range(coarse)], tmp, gather)
        ):
            outgoing[c] = value

    @pl.when(has_prev)
    def _():
        next_own.wait_recv()
        when(has_outer, next_out.wait_recv)
        next_in.wait_recv()
        for c in range(coarse):
            car[HALO_C + c] = car_own[c] - rs[HALO_C + c]
        for c in range(HALO_C):
            low, high = HALO_C - 1 - c, HALO_C + coarse + c
            car[low] = car_out[c] - rs[low]
            car[high] = car_in[HALO_C - 1 - c] - rs[high]
        steps = (car, ca, cb)
        for j, weight in enumerate(coarse_weights):
            beside = SWEEPS_C - 1 - j
            for c in range(-beside, coarse + beside):
                sweep_layer(
                    steps[j], car, steps[j + 1], cx, cy, cz, cinv, HALO_C + c, weight
                )

        @pl.when(has_next)
        def _():
            for c in range(coarse):
                outgoing[c] = outgoing[c] + cb[HALO_C + c]

    @pl.when(has_next)
    def _():
        when(has_outer, next_out.start)
        next_in.start()
        next_own.start()

    @pl.when(has_prev)
    def _():
        row_s = lax.broadcasted_iota(jnp.int32, (fine_y // 2, fine_y), 0)
        col_s = lax.broadcasted_iota(jnp.int32, (fine_y // 2, fine_y), 1)
        spread = jnp.where((col_s == 2 * row_s) | (col_s == 2 * row_s + 1), 1.0, 0.0)
        rows = tmp.shape[1]
        for c in range(coarse):
            for parity in range(2):
                tmp[c, pl.ds(parity, rows // 2, 2), :] = cb[HALO_C + c]
        wide = times_exact(jnp.concatenate([tmp[c] for c in range(coarse)], axis=0), spread)
        for u in range(layers):
            out[0, place(u)] = w6[at(u)] + wide[(u // 2) * rows : (u // 2 + 1) * rows]

    @pl.when(jnp.logical_not(has_prev))
    def _():
        for u in range(layers):
            out[0, place(u)] = w6[at(u)]

    for ok, copy in sent:
        when(ok, copy.wait_send)


def shards(states, conduct):
    cut_count, gz_count = lax.axis_size("cuts"), lax.axis_size("gz")
    layers, nx, ny = conduct.shape
    assert gz_count % 2 == 0 and layers % 2 == 0 and layers >= HALO
    fine = pltpu.VMEM((layers + 2 * HALO, nx, ny), jnp.float32)

    def small(count):
        return pltpu.VMEM((count, nx // 2, ny // 2), jnp.float32)

    copies = 5 * HALO + DEEP - 1 + SWEEPS + 3
    return pl.pallas_call(
        functools.partial(kernel, cut_count, gz_count, layers),
        out_shape=pltpu.VMEM(states.shape, jnp.float32),
        in_specs=[pl.BlockSpec(memory_space=pl.ANY)] * 2,
        out_specs=pl.BlockSpec(memory_space=pltpu.VMEM),
        scratch_shapes=[fine] * 12
        + [pltpu.VMEM((layers // 2 + 2 * HALO_C, nx, ny // 2), jnp.float32)]
        + [small(layers // 2 + 2 * HALO_C)] * 9
        + [small(layers // 2), small(HALO_C), small(HALO_C), small(layers // 2)]
        + [
            pltpu.SemaphoreType.DMA((2 * layers,)),
            pltpu.SemaphoreType.DMA((copies,)),
            pltpu.SemaphoreType.DMA((copies,)),
        ],
        compiler_params=pltpu.CompilerParams(collective_id=0, has_side_effects=True),
        name="parareal",
    )(states, conduct)


def solution(mesh):
    in_specs = (P("cuts", "gz", None, None), P("gz", None, None))
    out_specs = P("cuts", "gz", None, None)
    return jax.shard_map(shards, mesh=mesh, in_specs=in_specs, out_specs=out_specs, check_vma=False)
```

```python
import functools
import math

import jax
import jax.numpy as jnp
from jax import lax
from jax.experimental import pallas as pl
from jax.experimental.pallas import tpu as pltpu
from jax.sharding import PartitionSpec as P

STEPS = 2
SWEEPS = 3
SWEEPS_C = 2

COUPLING = 1.0
SPREAD = 0.85
MESH = pl.DeviceIdType.MESH

HALO = 4
HALO_C = HALO // 2
ROUNDS = STEPS * SWEEPS
DEEP = ROUNDS // 2
DIRECT = 2


def chebyshev_weights(count):
    return [
        1.0 / (1.0 + SPREAD * math.cos(math.pi * (2 * index_now + 1) / (2 * count)))
        for index_now in range(count)
    ]


def down(v, axis):
    return pltpu.roll(v, 1, axis)


def up(v, axis):
    return pltpu.roll(v, v.shape[axis] - 1, axis)


def coefficient_layer(k_ref, bx, by, inv, l, coupling, keep):
    shape = k_ref.shape[1:]
    at_x = lax.broadcasted_iota(jnp.int32, shape, 0)
    at_y = lax.broadcasted_iota(jnp.int32, shape, 1)
    half = 0.5 * coupling
    k = k_ref[l]
    x_lo = jnp.where(at_x == 0, 0.0, down(k, 0))
    x_hi = jnp.where(at_x == shape[0] - 1, 0.0, up(k, 0))
    y_lo = jnp.where(at_y == 0, 0.0, down(k, 1))
    y_hi = jnp.where(at_y == shape[1] - 1, 0.0, up(k, 1))
    bx[l] = jnp.where(at_x == 0, 0.0, half * (k + x_lo))
    by[l] = jnp.where(at_y == 0, 0.0, half * (k + y_lo))
    diag = 1.0 + half * (
        6.0 * k + (x_lo + x_hi) + (y_lo + y_hi) + (k_ref[l - 1] + k_ref[l + 1])
    )
    inv[l] = keep / diag


def sweep_layer(src, source, dst, bx, by, bz, inv, l, weight):
    w = src[l]
    b_y = by[l]
    b_x = bx[l]
    total = (
        source[l]
        + (b_y * down(w, 1) + up(b_y * w, 1))
        + (b_x * down(w, 0) + up(b_x * w, 0))
        + (bz[l] * src[l - 1] + bz[l + 1] * src[l + 1])
    )
    dst[l] = (1.0 - weight) * w + (weight * inv[l]) * total


def times_exact(value, matrix):
    high = value.astype(jnp.bfloat16)
    rest = value - high.astype(jnp.float32)
    middle = rest.astype(jnp.bfloat16)
    low = (rest - middle.astype(jnp.float32)).astype(jnp.bfloat16)
    count = value.shape[0]
    parts = lax.dot_general(
        jnp.concatenate([high, middle, low], axis=0),
        matrix.astype(jnp.bfloat16),
        (((1,), (0,)), ((), ())),
        preferred_element_type=jnp.float32,
    )
    return parts[:count] + (parts[count : 2 * count] + parts[2 * count :])


def restricted(field, firsts, tmp, matrix):
    rows = tmp.shape[1]
    sums = [field[first] + field[first + 1] for first in firsts]
    narrow = times_exact(jnp.concatenate(sums, axis=0), matrix)
    out = []
    for j in range(len(sums)):
        tmp[j] = narrow[j * rows : (j + 1) * rows]
        out.append(tmp[j, pl.ds(0, rows // 2, 2), :] + tmp[j, pl.ds(1, rows // 2, 2), :])
    return out


def kernel(
    cut_count, gz_count, layers,
    s_in, k_in, out,
    k, w0, w1, w2, w3, w4, w5, w6, bx, by, bz, inv, tmp,
    kc, cx, cy, cz, cinv, rs, car, ca, cb, car_own, car_out, car_in, outgoing,
    load_sem, send_sem, recv_sem, entered,
):
    cut = lax.axis_index("cuts")
    gz = lax.axis_index("gz")
    side = lax.rem(gz, 2)
    outer, inner = gz - 1 + 2 * side, gz + 1 - 2 * side
    has_outer = jnp.logical_and(outer >= 0, outer < gz_count)
    has_prev, has_next = cut > 0, cut < cut_count - 1
    odd = lax.rem(cut, 2) == 1
    relayed = jnp.logical_and(jnp.logical_not(odd), has_next)
    coarse = layers // 2
    always = None
    w = (w0, w1, w2, w3, w4, w5, w6)

    def at(u):
        return HALO + u

    def place(u):
        return u + side * (layers - 1 - 2 * u)

    def when(condition, act):
        if condition is always:
            act()
        else:
            pl.when(condition)(act)

    loads_k = [
        pltpu.make_async_copy(k_in.at[place(u)], k.at[at(u)], load_sem.at[u])
        for u in range(layers)
    ]
    loads_s = [
        pltpu.make_async_copy(s_in.at[0, place(u)], w0.at[at(u)], load_sem.at[layers + u])
        for u in range(layers)
    ]
    for load in loads_k + loads_s:
        load.start()

    barrier = pltpu.get_barrier_semaphore()
    for there, ok in (
        ((cut, outer), has_outer),
        ((cut, inner), always),
        ((cut + 1, gz), has_next),
    ):
        when(
            ok,
            lambda there=there: pl.semaphore_signal(
                barrier, inc=1, device_id=there, device_id_type=MESH
            ),
        )
    expected = 1 + has_outer.astype(jnp.int32) + has_prev.astype(jnp.int32)

    @pl.when(jnp.logical_not(has_outer))
    def _():
        fine = jnp.zeros((HALO,) + w0.shape[1:], jnp.float32)
        for ref in (w0, k):
            ref[pl.ds(0, HALO)] = fine
        for ref in (w1, w2):
            ref[0] = fine[0]
        car_out[...] = jnp.zeros(car_out.shape, jnp.float32)

    count = [0]
    sent = []

    def remote(src, dst, there, ok, slot=None):
        index = count[0]
        count[0] += 1
        copy = pltpu.make_async_remote_copy(
            src_ref=src,
            dst_ref=dst,
            send_sem=send_sem.at[index],
            recv_sem=recv_sem.at[index if slot is None else slot],
            device_id=there,
            device_id_type=MESH,
        )
        sent.append((ok, copy))
        return copy

    to_outer, to_inner = (cut, outer), (cut, inner)
    carries = jnp.logical_and(has_outer, jnp.logical_not(relayed))
    relays = jnp.logical_and(has_outer, odd)

    def own_k(u):
        return k_in.at[place(u)]

    def own_s(u):
        return s_in.at[0, place(u)]

    def mirrored(src, ref, u, ok):
        return remote(src, ref.at[at(-1 - u)], to_outer, ok)

    out_k = [
        mirrored(own_k(u), k, u, has_outer if u < DIRECT else carries) for u in range(HALO)
    ]
    out_w0 = [mirrored(own_s(u), w0, u, has_outer) for u in range(HALO)]
    out_w = {
        j: mirrored(w[j].at[at(HALO - 1)], w[j], HALO - 1, has_outer)
        for j in range(1, DEEP)
    }
    relay_k = [
        remote(k.at[at(-1 - u)], k.at[at(-1 - u)], (cut - 1, gz), relays, slot=u)
        for u in range(DIRECT, HALO)
    ]

    def across(src, ref, i):
        return remote(src, ref.at[at(layers + i)], to_inner, always)

    in_k = [across(own_k(layers - 1 - i), k, i) for i in range(HALO)]
    in_w0 = [across(own_s(layers - 1 - i), w0, i) for i in range(HALO)]
    in_half = [
        across(w[SWEEPS].at[at(layers - 1 - i)], w[SWEEPS], i) for i in range(SWEEPS)
    ]
    next_own = remote(outgoing, car_own, (cut + 1, gz), has_next)
    next_out = remote(
        outgoing.at[pl.ds(0, HALO_C)], car_out, (cut + 1, outer),
        jnp.logical_and(has_next, has_outer),
    )
    next_in = remote(
        outgoing.at[pl.ds(coarse - HALO_C, HALO_C)], car_in, (cut + 1, inner), has_next
    )

    keep_outer = jnp.where(has_outer, 1.0, 0.0)
    weights = chebyshev_weights(SWEEPS)
    coarse_weights = chebyshev_weights(SWEEPS_C)

    needed = []
    for j in range(1, ROUNDS + 1):
        low = -min(DEEP, ROUNDS - j)
        high = layers + (-j % SWEEPS)
        needed += [(j, u) for u in range(low, high)]
    waiting = dict.fromkeys(needed)
    have, have_k, faces, cells = set(), set(), set(), set()
    starts = {}
    early = jnp.logical_and(has_outer, jnp.logical_not(odd))
    for j, copy in out_w.items():
        starts[(j, HALO - 1)] = (early, copy)
    for i, copy in enumerate(in_half):
        starts[(SWEEPS, layers - 1 - i)] = (always, copy)

    def coefficients(u):
        for face in (u, u + 1):
            if face not in faces:
                bz[at(face)] = 0.5 * COUPLING * (k[at(face)] + k[at(face - 1)])
                faces.add(face)
        if u not in cells:
            coefficient_layer(k, bx, by, inv, at(u), COUPLING, keep_outer if u < 0 else 1.0)
            cells.add(u)

    def advance(values=(), conductivity=()):
        have.update(values)
        have_k.update(conductivity)
        for u in range(-DEEP, layers + SWEEPS - 1):
            if u not in cells and have_k >= {u - 1, u, u + 1}:
                coefficients(u)
        moved = True
        while moved:
            moved = False
            for j, u in list(waiting):
                first = SWEEPS * ((j - 1) // SWEEPS)
                inputs = {(j - 1, u - 1), (j - 1, u), (j - 1, u + 1), (first, u)}
                if u not in cells or not have >= inputs:
                    continue
                sweep_layer(
                    w[j - 1], w[first], w[j], bx, by, bz, inv, at(u),
                    weights[(j - 1) % SWEEPS],
                )
                have.add((j, u))
                del waiting[(j, u)]
                moved = True
                if (j, u) in starts:
                    ok, copy = starts[(j, u)]
                    when(ok, copy.start)

    pl.semaphore_wait(barrier, expected)

    when(
        has_prev,
        lambda: pl.semaphore_signal(
            entered, inc=1, device_id=(cut - 1, gz), device_id_type=MESH
        ),
    )
    k_order = [*range(DIRECT, HALO), *range(DIRECT)]
    for u in k_order:
        when(has_outer if u < DIRECT else carries, out_k[u].start)
    for copy in out_w0:
        when(early, copy.start)
    for a, b in zip(in_k, in_w0):
        a.start()
        b.start()

    for load in loads_k + loads_s:
        load.wait()
    advance([(0, u) for u in range(layers)], range(layers))
    for i in range(HALO):
        in_k[i].wait_recv()
        in_w0[i].wait_recv()
        advance([(0, layers + i)], [layers + i])

    fine_y = w0.shape[2]
    row = lax.broadcasted_iota(jnp.int32, (fine_y, fine_y // 2), 0)
    col = lax.broadcasted_iota(jnp.int32, (fine_y, fine_y // 2), 1)
    gather = jnp.where((row == 2 * col) | (row == 2 * col + 1), 0.125, 0.0)
    every_c = range(-HALO_C, coarse + HALO_C)

    @pl.when(has_prev)
    def _():
        for i, u in enumerate(k_order):
            when(has_outer, out_k[u].wait_recv)
            if u >= DIRECT:
                when(relays, relay_k[u - DIRECT].start)
            if i == 0:
                for copy in out_w0 + list(out_w.values()):
                    when(relays, copy.start)
        for c, value in zip(every_c, restricted(k, [at(2 * c) for c in every_c], tmp, gather)):
            kc[HALO_C + c] = value
        for c in range(-1, coarse + 2):
            cz[HALO_C + c] = 0.25 * COUPLING * (kc[HALO_C + c] + kc[HALO_C + c - 1])
        for c in range(-1, coarse + 1):
            coefficient_layer(
                kc, cx, cy, cinv, HALO_C + c, 0.5 * COUPLING, keep_outer if c < 0 else 1.0
            )

    first_waits = jnp.logical_and(has_outer, jnp.logical_not(has_prev))
    for u in range(HALO):
        when(first_waits, out_k[u].wait_recv)
        when(has_outer, out_w0[u].wait_recv)
        advance([(0, -1 - u)], [-1 - u])

    @pl.when(has_prev)
    def _():
        for c, value in zip(every_c, restricted(w0, [at(2 * c) for c in every_c], tmp, gather)):
            rs[HALO_C + c] = value

    for i in range(SWEEPS):
        in_half[i].wait_recv()
    advance([(SWEEPS, layers + i) for i in range(SWEEPS)])
    for j in range(1, DEEP):
        when(has_outer, out_w[j].wait_recv)
        advance([(j, -HALO)])

    @pl.when(has_next)
    def _():
        for c, value in enumerate(
            restricted(w6, [at(2 * c) for c in range(coarse)], tmp, gather)
        ):
            outgoing[c] = value

    @pl.when(has_prev)
    def _():
        next_own.wait_recv()
        when(has_outer, next_out.wait_recv)
        next_in.wait_recv()
        for c in range(coarse):
            car[HALO_C + c] = car_own[c] - rs[HALO_C + c]
        for c in range(HALO_C):
            low, high = HALO_C - 1 - c, HALO_C + coarse + c
            car[low] = car_out[c] - rs[low]
            car[high] = car_in[HALO_C - 1 - c] - rs[high]
        steps = (car, ca, cb)
        for j, weight in enumerate(coarse_weights):
            beside = SWEEPS_C - 1 - j
            for c in range(-beside, coarse + beside):
                sweep_layer(
                    steps[j], car, steps[j + 1], cx, cy, cz, cinv, HALO_C + c, weight
                )

        @pl.when(has_next)
        def _():
            for c in range(coarse):
                outgoing[c] = outgoing[c] + cb[HALO_C + c]

    @pl.when(has_next)
    def _():
        pl.semaphore_wait(entered, 1)
        when(has_outer, next_out.start)
        next_in.start()
        next_own.start()

    @pl.when(has_prev)
    def _():
        row_s = lax.broadcasted_iota(jnp.int32, (fine_y // 2, fine_y), 0)
        col_s = lax.broadcasted_iota(jnp.int32, (fine_y // 2, fine_y), 1)
        spread = jnp.where((col_s == 2 * row_s) | (col_s == 2 * row_s + 1), 1.0, 0.0)
        rows = tmp.shape[1]
        for c in range(coarse):
            for parity in range(2):
                tmp[c, pl.ds(parity, rows // 2, 2), :] = cb[HALO_C + c]
        wide = times_exact(jnp.concatenate([tmp[c] for c in range(coarse)], axis=0), spread)
        for u in range(layers):
            out[0, place(u)] = w6[at(u)] + wide[(u // 2) * rows : (u // 2 + 1) * rows]

    @pl.when(jnp.logical_not(has_prev))
    def _():
        for u in range(layers):
            out[0, place(u)] = w6[at(u)]

    for ok, copy in sent:
        when(ok, copy.wait_send)


def shards(states, conduct):
    cut_count, gz_count = lax.axis_size("cuts"), lax.axis_size("gz")
    layers, nx, ny = conduct.shape
    assert gz_count % 2 == 0 and layers % 2 == 0 and layers >= HALO
    fine = pltpu.VMEM((layers + 2 * HALO, nx, ny), jnp.float32)

    def small(count):
        return pltpu.VMEM((count, nx // 2, ny // 2), jnp.float32)

    copies = 5 * HALO - DIRECT + DEEP - 1 + SWEEPS + 3
    return pl.pallas_call(
        functools.partial(kernel, cut_count, gz_count, layers),
        out_shape=pltpu.VMEM(states.shape, jnp.float32),
        in_specs=[pl.BlockSpec(memory_space=pl.ANY)] * 2,
        out_specs=pl.BlockSpec(memory_space=pltpu.VMEM),
        scratch_shapes=[fine] * 12
        + [pltpu.VMEM((layers // 2 + 2 * HALO_C, nx, ny // 2), jnp.float32)]
        + [small(layers // 2 + 2 * HALO_C)] * 9
        + [small(layers // 2), small(HALO_C), small(HALO_C), small(layers // 2)]
        + [
            pltpu.SemaphoreType.DMA((2 * layers,)),
            pltpu.SemaphoreType.DMA((copies,)),
            pltpu.SemaphoreType.DMA((copies,)),
            pltpu.SemaphoreType.REGULAR,
        ],
        compiler_params=pltpu.CompilerParams(collective_id=0, has_side_effects=True),
        name="parareal",
    )(states, conduct)


def solution(mesh):
    in_specs = (P("cuts", "gz", None, None), P("gz", None, None))
    out_specs = P("cuts", "gz", None, None)
    return jax.shard_map(shards, mesh=mesh, in_specs=in_specs, out_specs=out_specs, check_vma=False)
```

```python
import functools
import math

import jax
import jax.numpy as jnp
from jax import lax
from jax.experimental import pallas as pl
from jax.experimental.pallas import tpu as pltpu
from jax.sharding import PartitionSpec as P

STEPS = 2
SWEEPS = 3
SWEEPS_C = 2

COUPLING = 1.0
SPREAD = 0.85
MESH = pl.DeviceIdType.MESH

HALO = 4
HALO_C = HALO // 2
ROUNDS = STEPS * SWEEPS
DEEP = ROUNDS // 2 - 1
EDGE = DEEP + 1
DIRECT = 2
PACE = 2
EDGES, HALF, DEEPER = "edge", "half", "deep"
GROUPS = (
    ((EDGES, 0),),
    ((EDGES, 1),),
    ((EDGES, 2), (HALF, None)),
    ((DEEPER, 1), (DEEPER, 2)),
    ((DEEPER, 3),),
)


def chebyshev_weights(count):
    return [
        1.0 / (1.0 + SPREAD * math.cos(math.pi * (2 * index_now + 1) / (2 * count)))
        for index_now in range(count)
    ]


def down(v, axis):
    return pltpu.roll(v, 1, axis)


def up(v, axis):
    return pltpu.roll(v, v.shape[axis] - 1, axis)


def coefficient_layer(k_ref, bx, by, inv, l, coupling, keep):
    shape = k_ref.shape[1:]
    at_x = lax.broadcasted_iota(jnp.int32, shape, 0)
    at_y = lax.broadcasted_iota(jnp.int32, shape, 1)
    half = 0.5 * coupling
    k = k_ref[l]
    x_lo = jnp.where(at_x == 0, 0.0, down(k, 0))
    x_hi = jnp.where(at_x == shape[0] - 1, 0.0, up(k, 0))
    y_lo = jnp.where(at_y == 0, 0.0, down(k, 1))
    y_hi = jnp.where(at_y == shape[1] - 1, 0.0, up(k, 1))
    bx[l] = jnp.where(at_x == 0, 0.0, half * (k + x_lo))
    by[l] = jnp.where(at_y == 0, 0.0, half * (k + y_lo))
    diag = 1.0 + half * (
        6.0 * k + (x_lo + x_hi) + (y_lo + y_hi) + (k_ref[l - 1] + k_ref[l + 1])
    )
    inv[l] = keep / diag


def sweep_layer(src, source, dst, bx, by, bz, inv, l, weight):
    w = src[l]
    b_y = by[l]
    b_x = bx[l]
    total = (
        source[l]
        + (b_y * down(w, 1) + up(b_y * w, 1))
        + (b_x * down(w, 0) + up(b_x * w, 0))
        + (bz[l] * src[l - 1] + bz[l + 1] * src[l + 1])
    )
    dst[l] = (1.0 - weight) * w + (weight * inv[l]) * total


def times_exact(value, matrix):
    high = value.astype(jnp.bfloat16)
    rest = value - high.astype(jnp.float32)
    middle = rest.astype(jnp.bfloat16)
    low = (rest - middle.astype(jnp.float32)).astype(jnp.bfloat16)
    count = value.shape[0]
    parts = lax.dot_general(
        jnp.concatenate([high, middle, low], axis=0),
        matrix.astype(jnp.bfloat16),
        (((1,), (0,)), ((), ())),
        preferred_element_type=jnp.float32,
    )
    return parts[:count] + (parts[count : 2 * count] + parts[2 * count :])


def restricted(pairs, tmp, matrix):
    rows = tmp.shape[1]
    sums = [field[first] + field[first + 1] for field, first in pairs]
    narrow = times_exact(jnp.concatenate(sums, axis=0), matrix)
    out = []
    for j in range(len(sums)):
        tmp[j] = narrow[j * rows : (j + 1) * rows]
        out.append(tmp[j, pl.ds(0, rows // 2, 2), :] + tmp[j, pl.ds(1, rows // 2, 2), :])
    return out


def kernel(
    cut_count, gz_count, layers,
    s_in, k_in, out,
    k, w0, w1, w2, w3, w4, w5, w6, bx, by, bz, inv, tmp,
    kc, cx, cy, cz, cinv, rs, car, ca, cb, shared, given, car_own, car_out, car_in, outgoing,
    load_sem, send_sem, recv_sem, entered,
):
    cut = lax.axis_index("cuts")
    gz = lax.axis_index("gz")
    side = lax.rem(gz, 2)
    outer, inner = gz - 1 + 2 * side, gz + 1 - 2 * side
    has_outer = jnp.logical_and(outer >= 0, outer < gz_count)
    has_prev, has_next = cut > 0, cut < cut_count - 1
    odd = lax.rem(cut, 2) == 1
    relayed = jnp.logical_and(jnp.logical_not(odd), has_next)
    coarse = layers // 2
    always = None
    w = (w0, w1, w2, w3, w4, w5, w6)

    def at(u):
        return HALO + u

    def place(u):
        return u + side * (layers - 1 - 2 * u)

    def when(condition, act):
        if condition is always:
            act()
        else:
            pl.when(condition)(act)

    loads_k = [
        pltpu.make_async_copy(k_in.at[place(u)], k.at[at(u)], load_sem.at[u])
        for u in range(layers)
    ]
    loads_s = [
        pltpu.make_async_copy(s_in.at[0, place(u)], w0.at[at(u)], load_sem.at[layers + u])
        for u in range(layers)
    ]
    for load in loads_k + loads_s:
        load.start()

    barrier = pltpu.get_barrier_semaphore()
    for there, ok in (
        ((cut, outer), has_outer),
        ((cut, inner), always),
        ((cut + 1, gz), has_next),
    ):
        when(
            ok,
            lambda there=there: pl.semaphore_signal(
                barrier, inc=1, device_id=there, device_id_type=MESH
            ),
        )
    expected = 1 + has_outer.astype(jnp.int32) + has_prev.astype(jnp.int32)

    @pl.when(jnp.logical_not(has_outer))
    def _():
        fine = jnp.zeros((EDGE,) + w0.shape[1:], jnp.float32)
        for ref in (w0, k):
            ref[pl.ds(at(-EDGE), EDGE)] = fine
        for j in range(1, ROUNDS - DEEP):
            w[j][at(-EDGE)] = fine[0]
        given[...] = jnp.zeros(given.shape, jnp.float32)
        car_out[...] = jnp.zeros(car_out.shape, jnp.float32)

    count = [0]
    sent = []

    def remote(src, dst, there, ok, slot=None):
        index = count[0]
        count[0] += 1
        copy = pltpu.make_async_remote_copy(
            src_ref=src,
            dst_ref=dst,
            send_sem=send_sem.at[index],
            recv_sem=recv_sem.at[index if slot is None else slot],
            device_id=there,
            device_id_type=MESH,
        )
        sent.append((ok, copy))
        return copy

    to_outer, to_inner = (cut, outer), (cut, inner)
    carries = jnp.logical_and(has_outer, jnp.logical_not(relayed))
    relays = jnp.logical_and(has_outer, odd)

    def own_k(u):
        return k_in.at[place(u)]

    def own_s(u):
        return s_in.at[0, place(u)]

    def mirrored(src, ref, u, ok):
        return remote(src, ref.at[at(-1 - u)], to_outer, ok)

    out_k = [
        mirrored(own_k(u), k, u, has_outer if u < DIRECT else carries) for u in range(EDGE)
    ]
    out_w0 = [mirrored(own_s(u), w0, u, has_outer) for u in range(EDGE)]
    out_w = {
        j: mirrored(w[j].at[at(DEEP)], w[j], DEEP, has_outer)
        for j in range(1, ROUNDS - DEEP)
    }
    relay_k = [
        remote(k.at[at(-1 - u)], k.at[at(-1 - u)], (cut - 1, gz), relays, slot=u)
        for u in range(DIRECT, EDGE)
    ]

    def across(src, ref, i):
        return remote(src, ref.at[at(layers + i)], to_inner, always)

    in_k = [across(own_k(layers - 1 - i), k, i) for i in range(HALO)]
    in_w0 = [across(own_s(layers - 1 - i), w0, i) for i in range(HALO)]
    in_half = [
        across(w[SWEEPS].at[at(layers - 1 - i)], w[SWEEPS], i) for i in range(SWEEPS)
    ]
    out_shared = remote(
        shared, given, to_outer, jnp.logical_and(has_prev, has_outer)
    )
    next_own = remote(outgoing, car_own, (cut + 1, gz), has_next)
    next_out = remote(
        outgoing.at[pl.ds(0, HALO_C)], car_out, (cut + 1, outer),
        jnp.logical_and(has_next, has_outer),
    )
    next_in = remote(
        outgoing.at[pl.ds(coarse - HALO_C, HALO_C)], car_in, (cut + 1, inner), has_next
    )

    keep_outer = jnp.where(has_outer, 1.0, 0.0)
    weights = chebyshev_weights(SWEEPS)
    coarse_weights = chebyshev_weights(SWEEPS_C)

    needed = []
    for j in range(1, ROUNDS + 1):
        low = -min(DEEP, ROUNDS - j)
        high = layers + (-j % SWEEPS)
        needed += [(j, u) for u in range(low, high)]
    waiting = dict.fromkeys(needed)
    have, have_k, faces, cells = set(), set(), set(), set()
    starts = {}
    early = jnp.logical_and(has_outer, jnp.logical_not(odd))
    for j, copy in out_w.items():
        starts.setdefault((j, DEEP), []).append((early if j <= DEEP else has_outer, copy))
    for i, copy in enumerate(in_half):
        starts.setdefault((SWEEPS, layers - 1 - i), []).append((always, copy))

    def coefficients(u):
        for face in (u, u + 1):
            if face not in faces:
                bz[at(face)] = 0.5 * COUPLING * (k[at(face)] + k[at(face - 1)])
                faces.add(face)
        if u not in cells:
            coefficient_layer(k, bx, by, inv, at(u), COUPLING, keep_outer if u < 0 else 1.0)
            cells.add(u)

    def advance(values=(), conductivity=()):
        have.update(values)
        have_k.update(conductivity)
        for u in range(-DEEP, layers + SWEEPS - 1):
            if u not in cells and have_k >= {u - 1, u, u + 1}:
                coefficients(u)
        moved, leaving = True, []
        while moved:
            moved = False
            for j, u in list(waiting):
                first = SWEEPS * ((j - 1) // SWEEPS)
                inputs = {(j - 1, u - 1), (j - 1, u), (j - 1, u + 1), (first, u)}
                if u not in cells or not have >= inputs:
                    continue
                sweep_layer(
                    w[j - 1], w[first], w[j], bx, by, bz, inv, at(u),
                    weights[(j - 1) % SWEEPS],
                )
                have.add((j, u))
                del waiting[(j, u)]
                moved = True
                leaving += starts.get((j, u), [])
        for ok, copy in leaving:
            when(ok, copy.start)

    pl.semaphore_wait(barrier, expected)

    when(
        has_prev,
        lambda: pl.semaphore_signal(
            entered, inc=1, device_id=(cut - 1, gz), device_id_type=MESH
        ),
    )
    k_order = [*range(DIRECT, EDGE), *range(DIRECT)]
    for copy in out_k[:1] + out_w0[:1]:
        when(early, copy.start)
    for u in k_order:
        when(carries if u >= DIRECT else relays, out_k[u].start)
        if u == 0:
            when(relays, out_w0[0].start)
    for a, b in zip(in_k, in_w0):
        a.start()
        b.start()

    for load in loads_k + loads_s:
        load.wait()
    for i in range(HALO):
        if i == PACE:
            for copy in out_k[1:DIRECT] + out_w0[1:]:
                when(early, copy.start)
        in_k[i].wait_recv()
        in_w0[i].wait_recv()
    advance([(0, u) for u in range(layers + HALO)], range(layers + HALO))

    fine_y = w0.shape[2]
    row = lax.broadcasted_iota(jnp.int32, (fine_y, fine_y // 2), 0)
    col = lax.broadcasted_iota(jnp.int32, (fine_y, fine_y // 2), 1)
    gather = jnp.where((row == 2 * col) | (row == 2 * col + 1), 0.125, 0.0)
    near_c = range(coarse + HALO_C)

    @pl.when(has_prev)
    def _():
        both = restricted(
            [(ref, at(2 * c)) for ref in (k, w0) for c in near_c], tmp, gather
        )
        for c in near_c:
            kc[HALO_C + c] = both[c]
            rs[HALO_C + c] = both[len(near_c) + c]
        shared[0] = both[HALO_C - 1]
        shared[1] = both[len(near_c) + HALO_C - 1]
        for i, u in enumerate(k_order):
            when(has_outer, out_k[u].wait_recv)
            if u >= DIRECT:
                when(relays, relay_k[u - DIRECT].start)
            if i == 0:
                for copy in out_w0[1:] + [out_w[j] for j in range(1, DEEP + 1)]:
                    when(relays, copy.start)
                when(has_outer, out_shared.start)

    first_waits = jnp.logical_and(has_outer, jnp.logical_not(has_prev))

    def arrival(what, index):
        if what == EDGES:
            when(first_waits, out_k[index].wait_recv)
            when(has_outer, out_w0[index].wait_recv)
            return [(0, -1 - index)], [-1 - index]
        if what == HALF:
            for copy in in_half:
                copy.wait_recv()
            return [(SWEEPS, layers + i) for i in range(SWEEPS)], []
        when(has_outer, out_w[index].wait_recv)
        return [(index, -EDGE)], []

    for group in GROUPS:
        arrived = [arrival(*one) for one in group]
        advance(sum((v for v, _ in arrived), []), sum((c for _, c in arrived), []))

    @pl.when(has_next)
    def _():
        for c, value in enumerate(
            restricted([(w6, at(2 * c)) for c in range(coarse)], tmp, gather)
        ):
            outgoing[c] = value

    @pl.when(has_prev)
    def _():
        kc[HALO_C - 1], rs[HALO_C - 1] = restricted(
            [(ref, at(-2)) for ref in (k, w0)], tmp, gather
        )
        when(has_outer, out_shared.wait_recv)
        kc[0], rs[0] = given[0], given[1]
        for c in range(-1, coarse + 2):
            cz[HALO_C + c] = 0.25 * COUPLING * (kc[HALO_C + c] + kc[HALO_C + c - 1])
        for c in range(-1, coarse + 1):
            coefficient_layer(
                kc, cx, cy, cinv, HALO_C + c, 0.5 * COUPLING, keep_outer if c < 0 else 1.0
            )
        next_own.wait_recv()
        when(has_outer, next_out.wait_recv)
        next_in.wait_recv()
        for c in range(coarse):
            car[HALO_C + c] = car_own[c] - rs[HALO_C + c]
        for c in range(HALO_C):
            low, high = HALO_C - 1 - c, HALO_C + coarse + c
            car[low] = car_out[c] - rs[low]
            car[high] = car_in[HALO_C - 1 - c] - rs[high]
        steps = (car, ca, cb)
        for j, weight in enumerate(coarse_weights):
            beside = SWEEPS_C - 1 - j
            for c in range(-beside, coarse + beside):
                sweep_layer(
                    steps[j], car, steps[j + 1], cx, cy, cz, cinv, HALO_C + c, weight
                )

        @pl.when(has_next)
        def _():
            for c in range(coarse):
                outgoing[c] = outgoing[c] + cb[HALO_C + c]

    @pl.when(has_next)
    def _():
        pl.semaphore_wait(entered, 1)
        when(has_outer, next_out.start)
        next_in.start()
        next_own.start()

    @pl.when(has_prev)
    def _():
        row_s = lax.broadcasted_iota(jnp.int32, (fine_y // 2, fine_y), 0)
        col_s = lax.broadcasted_iota(jnp.int32, (fine_y // 2, fine_y), 1)
        spread = jnp.where((col_s == 2 * row_s) | (col_s == 2 * row_s + 1), 1.0, 0.0)
        rows = tmp.shape[1]
        for c in range(coarse):
            for parity in range(2):
                tmp[c, pl.ds(parity, rows // 2, 2), :] = cb[HALO_C + c]
        wide = times_exact(jnp.concatenate([tmp[c] for c in range(coarse)], axis=0), spread)
        for u in range(layers):
            out[0, place(u)] = w6[at(u)] + wide[(u // 2) * rows : (u // 2 + 1) * rows]

    @pl.when(jnp.logical_not(has_prev))
    def _():
        for u in range(layers):
            out[0, place(u)] = w6[at(u)]

    for ok, copy in sent:
        when(ok, copy.wait_send)


def shards(states, conduct):
    cut_count, gz_count = lax.axis_size("cuts"), lax.axis_size("gz")
    layers, nx, ny = conduct.shape
    assert gz_count % 2 == 0 and layers % 2 == 0 and layers >= HALO
    fine = pltpu.VMEM((layers + 2 * HALO, nx, ny), jnp.float32)

    def small(count):
        return pltpu.VMEM((count, nx // 2, ny // 2), jnp.float32)

    copies = 2 * HALO + 3 * EDGE - DIRECT + ROUNDS - DEEP - 1 + SWEEPS + 4
    return pl.pallas_call(
        functools.partial(kernel, cut_count, gz_count, layers),
        out_shape=pltpu.VMEM(states.shape, jnp.float32),
        in_specs=[pl.BlockSpec(memory_space=pl.ANY)] * 2,
        out_specs=pl.BlockSpec(memory_space=pltpu.VMEM),
        scratch_shapes=[fine] * 12
        + [pltpu.VMEM((layers + 2 * HALO_C, nx, ny // 2), jnp.float32)]
        + [small(layers // 2 + 2 * HALO_C)] * 9
        + [small(2), small(2)]
        + [small(layers // 2), small(HALO_C), small(HALO_C), small(layers // 2)]
        + [
            pltpu.SemaphoreType.DMA((2 * layers,)),
            pltpu.SemaphoreType.DMA((copies,)),
            pltpu.SemaphoreType.DMA((copies,)),
            pltpu.SemaphoreType.REGULAR,
        ],
        compiler_params=pltpu.CompilerParams(collective_id=0, has_side_effects=True),
        name="parareal",
    )(states, conduct)


def solution(mesh):
    in_specs = (P("cuts", "gz", None, None), P("gz", None, None))
    out_specs = P("cuts", "gz", None, None)
    return jax.shard_map(shards, mesh=mesh, in_specs=in_specs, out_specs=out_specs, check_vma=False)
```

```python
import functools
import math

import jax
import jax.numpy as jnp
from jax import lax
from jax.experimental import pallas as pl
from jax.experimental.pallas import tpu as pltpu
from jax.sharding import PartitionSpec as P

STEPS = 2
SWEEPS = 3
SWEEPS_C = 2

COUPLING = 1.0
SPREAD = 0.85
MESH = pl.DeviceIdType.MESH

HALO = 4
HALO_C = HALO // 2
ROUNDS = STEPS * SWEEPS
DEEP = ROUNDS // 2 - 1
EDGE = DEEP + 1
DIRECT = 2
PACE = 2
EDGES, HALF, DEEPER = "edge", "half", "deep"
GROUPS = (
    ((EDGES, 0),),
    ((EDGES, 1),),
    ((EDGES, 2), (HALF, None)),
    ((DEEPER, 1), (DEEPER, 2)),
    ((DEEPER, 3),),
)


def chebyshev_weights(count):
    return [
        1.0 / (1.0 + SPREAD * math.cos(math.pi * (2 * index_now + 1) / (2 * count)))
        for index_now in range(count)
    ]


def down(v, axis):
    return pltpu.roll(v, 1, axis)


def up(v, axis):
    return pltpu.roll(v, v.shape[axis] - 1, axis)


def coefficient_layer(k_ref, bx, by, inv, l, coupling, keep):
    shape = k_ref.shape[1:]
    at_x = lax.broadcasted_iota(jnp.int32, shape, 0)
    at_y = lax.broadcasted_iota(jnp.int32, shape, 1)
    half = 0.5 * coupling
    k = k_ref[l]
    x_lo = jnp.where(at_x == 0, 0.0, down(k, 0))
    x_hi = jnp.where(at_x == shape[0] - 1, 0.0, up(k, 0))
    y_lo = jnp.where(at_y == 0, 0.0, down(k, 1))
    y_hi = jnp.where(at_y == shape[1] - 1, 0.0, up(k, 1))
    bx[l] = jnp.where(at_x == 0, 0.0, half * (k + x_lo))
    by[l] = jnp.where(at_y == 0, 0.0, half * (k + y_lo))
    diag = 1.0 + half * (
        6.0 * k + (x_lo + x_hi) + (y_lo + y_hi) + (k_ref[l - 1] + k_ref[l + 1])
    )
    inv[l] = keep / diag


def sweep_layer(src, source, dst, bx, by, bz, inv, l, weight):
    w = src[l]
    b_y = by[l]
    b_x = bx[l]
    total = (
        source[l]
        + (b_y * down(w, 1) + up(b_y * w, 1))
        + (b_x * down(w, 0) + up(b_x * w, 0))
        + (bz[l] * src[l - 1] + bz[l + 1] * src[l + 1])
    )
    dst[l] = (1.0 - weight) * w + (weight * inv[l]) * total


def lanes(v, index):
    return jnp.take_along_axis(v, index, axis=1)


def restricted(pairs, tmp):
    rows = tmp.shape[1]
    width = tmp.shape[2]
    lane = lax.broadcasted_iota(jnp.int32, (rows, width), 1)
    even = lax.rem(2 * lane, width)
    out = []
    for j, (field, first) in enumerate(pairs):
        v = field[first] + field[first + 1]
        v = 0.125 * (v + up(v, 1))
        tmp[j] = jnp.where(lane < width // 2, lanes(v[:, :width], even), lanes(v[:, width:], even))
        out.append(tmp[j, pl.ds(0, rows // 2, 2), :] + tmp[j, pl.ds(1, rows // 2, 2), :])
    return out


def kernel(
    cut_count, gz_count, layers,
    s_in, k_in, out,
    k, w0, w1, w2, w3, w4, w5, w6, bx, by, bz, inv, tmp,
    kc, cx, cy, cz, cinv, rs, car, ca, cb, shared, given, car_own, car_out, car_in, outgoing,
    load_sem, send_sem, recv_sem, entered,
):
    cut = lax.axis_index("cuts")
    gz = lax.axis_index("gz")
    side = lax.rem(gz, 2)
    outer, inner = gz - 1 + 2 * side, gz + 1 - 2 * side
    has_outer = jnp.logical_and(outer >= 0, outer < gz_count)
    has_prev, has_next = cut > 0, cut < cut_count - 1
    odd = lax.rem(cut, 2) == 1
    relayed = jnp.logical_and(jnp.logical_not(odd), has_next)
    coarse = layers // 2
    always = None
    w = (w0, w1, w2, w3, w4, w5, w6)

    def at(u):
        return HALO + u

    def place(u):
        return u + side * (layers - 1 - 2 * u)

    def when(condition, act):
        if condition is always:
            act()
        else:
            pl.when(condition)(act)

    loads_k = [
        pltpu.make_async_copy(k_in.at[place(u)], k.at[at(u)], load_sem.at[u])
        for u in range(layers)
    ]
    loads_s = [
        pltpu.make_async_copy(s_in.at[0, place(u)], w0.at[at(u)], load_sem.at[layers + u])
        for u in range(layers)
    ]
    for load in loads_k + loads_s:
        load.start()

    barrier = pltpu.get_barrier_semaphore()
    for there, ok in (
        ((cut, outer), has_outer),
        ((cut, inner), always),
        ((cut + 1, gz), has_next),
    ):
        when(
            ok,
            lambda there=there: pl.semaphore_signal(
                barrier, inc=1, device_id=there, device_id_type=MESH
            ),
        )
    expected = 1 + has_outer.astype(jnp.int32) + has_prev.astype(jnp.int32)

    @pl.when(jnp.logical_not(has_outer))
    def _():
        fine = jnp.zeros((EDGE,) + w0.shape[1:], jnp.float32)
        for ref in (w0, k):
            ref[pl.ds(at(-EDGE), EDGE)] = fine
        for j in range(1, ROUNDS - DEEP):
            w[j][at(-EDGE)] = fine[0]
        given[...] = jnp.zeros(given.shape, jnp.float32)
        car_out[...] = jnp.zeros(car_out.shape, jnp.float32)

    count = [0]
    sent = []

    def remote(src, dst, there, ok, slot=None):
        index = count[0]
        count[0] += 1
        copy = pltpu.make_async_remote_copy(
            src_ref=src,
            dst_ref=dst,
            send_sem=send_sem.at[index],
            recv_sem=recv_sem.at[index if slot is None else slot],
            device_id=there,
            device_id_type=MESH,
        )
        sent.append((ok, copy))
        return copy

    to_outer, to_inner = (cut, outer), (cut, inner)
    carries = jnp.logical_and(has_outer, jnp.logical_not(relayed))
    relays = jnp.logical_and(has_outer, odd)

    def own_k(u):
        return k_in.at[place(u)]

    def own_s(u):
        return s_in.at[0, place(u)]

    def mirrored(src, ref, u, ok):
        return remote(src, ref.at[at(-1 - u)], to_outer, ok)

    out_k = [
        mirrored(own_k(u), k, u, has_outer if u < DIRECT else carries) for u in range(EDGE)
    ]
    out_w0 = [mirrored(own_s(u), w0, u, has_outer) for u in range(EDGE)]
    out_w = {
        j: mirrored(w[j].at[at(DEEP)], w[j], DEEP, has_outer)
        for j in range(1, ROUNDS - DEEP)
    }
    relay_k = [
        remote(k.at[at(-1 - u)], k.at[at(-1 - u)], (cut - 1, gz), relays, slot=u)
        for u in range(DIRECT, EDGE)
    ]

    def across(src, ref, i):
        return remote(src, ref.at[at(layers + i)], to_inner, always)

    in_k = [across(own_k(layers - 1 - i), k, i) for i in range(HALO)]
    in_w0 = [across(own_s(layers - 1 - i), w0, i) for i in range(HALO)]
    in_half = [
        across(w[SWEEPS].at[at(layers - 1 - i)], w[SWEEPS], i) for i in range(SWEEPS)
    ]
    out_shared = remote(
        shared, given, to_outer, jnp.logical_and(has_prev, has_outer)
    )
    next_own = remote(outgoing, car_own, (cut + 1, gz), has_next)
    next_out = remote(
        outgoing.at[pl.ds(0, HALO_C)], car_out, (cut + 1, outer),
        jnp.logical_and(has_next, has_outer),
    )
    next_in = remote(
        outgoing.at[pl.ds(coarse - HALO_C, HALO_C)], car_in, (cut + 1, inner), has_next
    )

    keep_outer = jnp.where(has_outer, 1.0, 0.0)
    weights = chebyshev_weights(SWEEPS)
    coarse_weights = chebyshev_weights(SWEEPS_C)

    needed = []
    for j in range(1, ROUNDS + 1):
        low = -min(DEEP, ROUNDS - j)
        high = layers + (-j % SWEEPS)
        needed += [(j, u) for u in range(low, high)]
    waiting = dict.fromkeys(needed)
    have, have_k, faces, cells = set(), set(), set(), set()
    starts = {}
    early = jnp.logical_and(has_outer, jnp.logical_not(odd))
    for j, copy in out_w.items():
        starts.setdefault((j, DEEP), []).append((early if j <= DEEP else has_outer, copy))
    for i, copy in enumerate(in_half):
        starts.setdefault((SWEEPS, layers - 1 - i), []).append((always, copy))

    def coefficients(u):
        for face in (u, u + 1):
            if face not in faces:
                bz[at(face)] = 0.5 * COUPLING * (k[at(face)] + k[at(face - 1)])
                faces.add(face)
        if u not in cells:
            coefficient_layer(k, bx, by, inv, at(u), COUPLING, keep_outer if u < 0 else 1.0)
            cells.add(u)

    def advance(values=(), conductivity=()):
        have.update(values)
        have_k.update(conductivity)
        for u in range(-DEEP, layers + SWEEPS - 1):
            if u not in cells and have_k >= {u - 1, u, u + 1}:
                coefficients(u)
        moved, leaving = True, []
        while moved:
            moved = False
            for j, u in list(waiting):
                first = SWEEPS * ((j - 1) // SWEEPS)
                inputs = {(j - 1, u - 1), (j - 1, u), (j - 1, u + 1), (first, u)}
                if u not in cells or not have >= inputs:
                    continue
                sweep_layer(
                    w[j - 1], w[first], w[j], bx, by, bz, inv, at(u),
                    weights[(j - 1) % SWEEPS],
                )
                have.add((j, u))
                del waiting[(j, u)]
                moved = True
                leaving += starts.get((j, u), [])
        for ok, copy in leaving:
            when(ok, copy.start)

    pl.semaphore_wait(barrier, expected)

    when(
        has_prev,
        lambda: pl.semaphore_signal(
            entered, inc=1, device_id=(cut - 1, gz), device_id_type=MESH
        ),
    )
    k_order = [*range(DIRECT, EDGE), *range(DIRECT)]
    for copy in out_k[:1] + out_w0[:1]:
        when(early, copy.start)
    for u in k_order:
        when(carries if u >= DIRECT else relays, out_k[u].start)
        if u == 0:
            when(relays, out_w0[0].start)
    for a, b in zip(in_k, in_w0):
        a.start()
        b.start()

    for load in loads_k + loads_s:
        load.wait()
    for i in range(HALO):
        if i == PACE:
            for copy in out_k[1:DIRECT] + out_w0[1:]:
                when(early, copy.start)
        in_k[i].wait_recv()
        in_w0[i].wait_recv()
    advance([(0, u) for u in range(layers + HALO)], range(layers + HALO))

    near_c = range(coarse + HALO_C)

    @pl.when(has_prev)
    def _():
        both = restricted(
            [(ref, at(2 * c)) for ref in (k, w0) for c in near_c], tmp
        )
        for c in near_c:
            kc[HALO_C + c] = both[c]
            rs[HALO_C + c] = both[len(near_c) + c]
        shared[0] = both[HALO_C - 1]
        shared[1] = both[len(near_c) + HALO_C - 1]
        for i, u in enumerate(k_order):
            when(has_outer, out_k[u].wait_recv)
            if u >= DIRECT:
                when(relays, relay_k[u - DIRECT].start)
            if i == 0:
                for copy in out_w0[1:] + [out_w[j] for j in range(1, DEEP + 1)]:
                    when(relays, copy.start)
                when(has_outer, out_shared.start)

    first_waits = jnp.logical_and(has_outer, jnp.logical_not(has_prev))

    def arrival(what, index):
        if what == EDGES:
            when(first_waits, out_k[index].wait_recv)
            when(has_outer, out_w0[index].wait_recv)
            return [(0, -1 - index)], [-1 - index]
        if what == HALF:
            for copy in in_half:
                copy.wait_recv()
            return [(SWEEPS, layers + i) for i in range(SWEEPS)], []
        when(has_outer, out_w[index].wait_recv)
        return [(index, -EDGE)], []

    for group in GROUPS:
        arrived = [arrival(*one) for one in group]
        advance(sum((v for v, _ in arrived), []), sum((c for _, c in arrived), []))

    @pl.when(has_next)
    def _():
        for c, value in enumerate(
            restricted([(w6, at(2 * c)) for c in range(coarse)], tmp)
        ):
            outgoing[c] = value

    @pl.when(has_prev)
    def _():
        kc[HALO_C - 1], rs[HALO_C - 1] = restricted(
            [(ref, at(-2)) for ref in (k, w0)], tmp
        )
        when(has_outer, out_shared.wait_recv)
        kc[0], rs[0] = given[0], given[1]
        for c in range(-1, coarse + 2):
            cz[HALO_C + c] = 0.25 * COUPLING * (kc[HALO_C + c] + kc[HALO_C + c - 1])
        for c in range(-1, coarse + 1):
            coefficient_layer(
                kc, cx, cy, cinv, HALO_C + c, 0.5 * COUPLING, keep_outer if c < 0 else 1.0
            )
        next_own.wait_recv()
        when(has_outer, next_out.wait_recv)
        next_in.wait_recv()
        for c in range(coarse):
            car[HALO_C + c] = car_own[c] - rs[HALO_C + c]
        for c in range(HALO_C):
            low, high = HALO_C - 1 - c, HALO_C + coarse + c
            car[low] = car_out[c] - rs[low]
            car[high] = car_in[HALO_C - 1 - c] - rs[high]
        steps = (car, ca, cb)
        for j, weight in enumerate(coarse_weights):
            beside = SWEEPS_C - 1 - j
            for c in range(-beside, coarse + beside):
                sweep_layer(
                    steps[j], car, steps[j + 1], cx, cy, cz, cinv, HALO_C + c, weight
                )

        @pl.when(has_next)
        def _():
            for c in range(coarse):
                outgoing[c] = outgoing[c] + cb[HALO_C + c]

    @pl.when(has_next)
    def _():
        pl.semaphore_wait(entered, 1)
        when(has_outer, next_out.start)
        next_in.start()
        next_own.start()

    @pl.when(has_prev)
    def _():
        rows = tmp.shape[1]
        for c in range(coarse):
            for parity in range(2):
                tmp[c, pl.ds(parity, rows // 2, 2), :] = cb[HALO_C + c]
        half = tmp.shape[2] // 2
        lane = lax.broadcasted_iota(jnp.int32, tmp.shape[1:], 1) // 2
        wide = jnp.concatenate(
            [
                jnp.concatenate([lanes(tmp[c], lane), lanes(tmp[c], lane + half)], axis=1)
                for c in range(coarse)
            ],
            axis=0,
        )
        for u in range(layers):
            out[0, place(u)] = w6[at(u)] + wide[(u // 2) * rows : (u // 2 + 1) * rows]

    @pl.when(jnp.logical_not(has_prev))
    def _():
        for u in range(layers):
            out[0, place(u)] = w6[at(u)]

    for ok, copy in sent:
        when(ok, copy.wait_send)


def shards(states, conduct):
    cut_count, gz_count = lax.axis_size("cuts"), lax.axis_size("gz")
    layers, nx, ny = conduct.shape
    assert gz_count % 2 == 0 and layers % 2 == 0 and layers >= HALO
    fine = pltpu.VMEM((layers + 2 * HALO, nx, ny), jnp.float32)

    def small(count):
        return pltpu.VMEM((count, nx // 2, ny // 2), jnp.float32)

    copies = 2 * HALO + 3 * EDGE - DIRECT + ROUNDS - DEEP - 1 + SWEEPS + 4
    return pl.pallas_call(
        functools.partial(kernel, cut_count, gz_count, layers),
        out_shape=pltpu.VMEM(states.shape, jnp.float32),
        in_specs=[pl.BlockSpec(memory_space=pl.ANY)] * 2,
        out_specs=pl.BlockSpec(memory_space=pltpu.VMEM),
        scratch_shapes=[fine] * 12
        + [pltpu.VMEM((layers + 2 * HALO_C, nx, ny // 2), jnp.float32)]
        + [small(layers // 2 + 2 * HALO_C)] * 9
        + [small(2), small(2)]
        + [small(layers // 2), small(HALO_C), small(HALO_C), small(layers // 2)]
        + [
            pltpu.SemaphoreType.DMA((2 * layers,)),
            pltpu.SemaphoreType.DMA((copies,)),
            pltpu.SemaphoreType.DMA((copies,)),
            pltpu.SemaphoreType.REGULAR,
        ],
        compiler_params=pltpu.CompilerParams(collective_id=0, has_side_effects=True),
        name="parareal",
    )(states, conduct)


def solution(mesh):
    in_specs = (P("cuts", "gz", None, None), P("gz", None, None))
    out_specs = P("cuts", "gz", None, None)
    return jax.shard_map(shards, mesh=mesh, in_specs=in_specs, out_specs=out_specs, check_vma=False)
```

```python
import functools
import math

import jax
import jax.numpy as jnp
from jax import lax
from jax.experimental import pallas as pl
from jax.experimental.pallas import tpu as pltpu
from jax.sharding import PartitionSpec as P

STEPS = 2
SWEEPS = 3
SWEEPS_C = 2

COUPLING = 1.0
SPREAD = 0.85
MESH = pl.DeviceIdType.MESH

HALO = 4
HALO_C = HALO // 2
ROUNDS = STEPS * SWEEPS
DEEP = ROUNDS // 2 - 1
EDGE = DEEP + 1
SHARE = 12
PACE = 2
EDGES, HALF, DEEPER = "edge", "half", "deep"
GROUPS = (
    ((EDGES, 0),),
    ((EDGES, 1),),
    ((HALF, None),),
    ((EDGES, 2),),
    ((DEEPER, 1), (DEEPER, 2)),
    ((DEEPER, 3),),
)


def chebyshev_weights(count):
    return [
        1.0 / (1.0 + SPREAD * math.cos(math.pi * (2 * index_now + 1) / (2 * count)))
        for index_now in range(count)
    ]


def down(v, axis):
    return pltpu.roll(v, 1, axis)


def up(v, axis):
    return pltpu.roll(v, v.shape[axis] - 1, axis)


def coefficient_layer(k_ref, bx, by, inv, l, coupling, keep):
    shape = k_ref.shape[1:]
    at_x = lax.broadcasted_iota(jnp.int32, shape, 0)
    at_y = lax.broadcasted_iota(jnp.int32, shape, 1)
    half = 0.5 * coupling
    k = k_ref[l]
    x_lo = jnp.where(at_x == 0, 0.0, down(k, 0))
    x_hi = jnp.where(at_x == shape[0] - 1, 0.0, up(k, 0))
    y_lo = jnp.where(at_y == 0, 0.0, down(k, 1))
    y_hi = jnp.where(at_y == shape[1] - 1, 0.0, up(k, 1))
    bx[l] = jnp.where(at_x == 0, 0.0, half * (k + x_lo))
    by[l] = jnp.where(at_y == 0, 0.0, half * (k + y_lo))
    diag = 1.0 + half * (
        6.0 * k + (x_lo + x_hi) + (y_lo + y_hi) + (k_ref[l - 1] + k_ref[l + 1])
    )
    inv[l] = keep / diag


def sweep_layer(src, source, dst, bx, by, bz, inv, l, weight):
    w = src[l]
    b_y = by[l]
    b_x = bx[l]
    total = (
        source[l]
        + (b_y * down(w, 1) + up(b_y * w, 1))
        + (b_x * down(w, 0) + up(b_x * w, 0))
        + (bz[l] * src[l - 1] + bz[l + 1] * src[l + 1])
    )
    dst[l] = (1.0 - weight) * w + (weight * inv[l]) * total


def lanes(v, index):
    return jnp.take_along_axis(v, index, axis=1)


def restricted(pairs, tmp):
    rows = tmp.shape[1]
    width = tmp.shape[2]
    lane = lax.broadcasted_iota(jnp.int32, (rows, width), 1)
    even = lax.rem(2 * lane, width)
    out = []
    for j, (field, first) in enumerate(pairs):
        v = field[first] + field[first + 1]
        v = 0.125 * (v + up(v, 1))
        tmp[j] = jnp.where(lane < width // 2, lanes(v[:, :width], even), lanes(v[:, width:], even))
        out.append(tmp[j, pl.ds(0, rows // 2, 2), :] + tmp[j, pl.ds(1, rows // 2, 2), :])
    return out


def kernel(
    cut_count, gz_count, layers,
    s_in, k_in, out,
    k, w0, w1, w2, w3, w4, w5, w6, bx, by, bz, inv, tmp,
    kc, cx, cy, cz, cinv, rs, car, ca, cb, shared, given, car_own, car_out, car_in, outgoing,
    load_sem, send_sem, recv_sem, entered,
):
    cut = lax.axis_index("cuts")
    gz = lax.axis_index("gz")
    side = lax.rem(gz, 2)
    outer, inner = gz - 1 + 2 * side, gz + 1 - 2 * side
    has_outer = jnp.logical_and(outer >= 0, outer < gz_count)
    has_prev, has_next = cut > 0, cut < cut_count - 1
    odd = lax.rem(cut, 2) == 1
    relayed = jnp.logical_and(jnp.logical_not(odd), has_next)
    coarse = layers // 2
    always = None
    w = (w0, w1, w2, w3, w4, w5, w6)

    def at(u):
        return HALO + u

    def place(u):
        return u + side * (layers - 1 - 2 * u)

    def when(condition, act):
        if condition is always:
            act()
        else:
            pl.when(condition)(act)

    loads_k = [
        pltpu.make_async_copy(k_in.at[place(u)], k.at[at(u)], load_sem.at[u])
        for u in range(layers)
    ]
    loads_s = [
        pltpu.make_async_copy(s_in.at[0, place(u)], w0.at[at(u)], load_sem.at[layers + u])
        for u in range(layers)
    ]
    for load in loads_k + loads_s:
        load.start()

    barrier = pltpu.get_barrier_semaphore()
    for there, ok in (
        ((cut, outer), has_outer),
        ((cut, inner), always),
        ((cut + 1, gz), has_next),
    ):
        when(
            ok,
            lambda there=there: pl.semaphore_signal(
                barrier, inc=1, device_id=there, device_id_type=MESH
            ),
        )
    expected = 1 + has_outer.astype(jnp.int32) + has_prev.astype(jnp.int32)

    @pl.when(jnp.logical_not(has_outer))
    def _():
        fine = jnp.zeros((EDGE,) + w0.shape[1:], jnp.float32)
        for ref in (w0, k):
            ref[pl.ds(at(-EDGE), EDGE)] = fine
        for j in range(1, ROUNDS - DEEP):
            w[j][at(-EDGE)] = fine[0]
        given[...] = jnp.zeros(given.shape, jnp.float32)
        car_out[...] = jnp.zeros(car_out.shape, jnp.float32)

    count = [0]
    sent = []

    def remote(src, dst, there, ok, slot=None):
        index = count[0]
        count[0] += 1
        copy = pltpu.make_async_remote_copy(
            src_ref=src,
            dst_ref=dst,
            send_sem=send_sem.at[index],
            recv_sem=recv_sem.at[index if slot is None else slot],
            device_id=there,
            device_id_type=MESH,
        )
        sent.append((ok, copy))
        return copy

    to_outer, to_inner = (cut, outer), (cut, inner)
    carries = jnp.logical_and(has_outer, jnp.logical_not(relayed))
    relays = jnp.logical_and(has_outer, odd)

    def own_k(u):
        return k_in.at[place(u)]

    def own_s(u):
        return s_in.at[0, place(u)]

    def mirrored(src, ref, u, ok):
        return remote(src, ref.at[at(-1 - u)], to_outer, ok)

    rows = w0.shape[1]
    cut_at = SHARE * rows // 16
    pieces = [(0, 0, rows), (1, 0, cut_at), (1, cut_at, rows - cut_at)]
    pieces += [(u, 0, rows) for u in range(2, EDGE)]
    direct = 2
    pieces_k = range(len(pieces))

    def piece(ref, i):
        return ref.at[pl.ds(*pieces[i][1:])]

    out_k = [
        remote(
            piece(own_k(pieces[i][0]), i), piece(k.at[at(-1 - pieces[i][0])], i),
            to_outer, has_outer if i < direct else carries,
        )
        for i in pieces_k
    ]
    out_w0 = [mirrored(own_s(u), w0, u, has_outer) for u in range(EDGE)]
    out_w = {
        j: mirrored(w[j].at[at(DEEP)], w[j], DEEP, has_outer)
        for j in range(1, ROUNDS - DEEP)
    }
    relay_k = [
        remote(
            piece(k.at[at(-1 - pieces[i][0])], i), piece(k.at[at(-1 - pieces[i][0])], i),
            (cut - 1, gz), relays, slot=i,
        )
        for i in pieces_k[direct:]
    ]

    def across(src, ref, i):
        return remote(src, ref.at[at(layers + i)], to_inner, always)

    in_k = [across(own_k(layers - 1 - i), k, i) for i in range(HALO)]
    in_w0 = [across(own_s(layers - 1 - i), w0, i) for i in range(HALO)]
    in_half = [
        across(w[SWEEPS].at[at(layers - 1 - i)], w[SWEEPS], i) for i in range(SWEEPS)
    ]
    out_shared = remote(
        shared, given, to_outer, jnp.logical_and(has_prev, has_outer)
    )
    next_own = remote(outgoing, car_own, (cut + 1, gz), has_next)
    next_out = remote(
        outgoing.at[pl.ds(0, HALO_C)], car_out, (cut + 1, outer),
        jnp.logical_and(has_next, has_outer),
    )
    next_in = remote(
        outgoing.at[pl.ds(coarse - HALO_C, HALO_C)], car_in, (cut + 1, inner), has_next
    )

    keep_outer = jnp.where(has_outer, 1.0, 0.0)
    weights = chebyshev_weights(SWEEPS)
    coarse_weights = chebyshev_weights(SWEEPS_C)

    needed = []
    for j in range(1, ROUNDS + 1):
        low = -min(DEEP, ROUNDS - j)
        high = layers + (-j % SWEEPS)
        needed += [(j, u) for u in range(low, high)]
    waiting = dict.fromkeys(needed)
    have, have_k, faces, cells = set(), set(), set(), set()
    starts = {}
    early = jnp.logical_and(has_outer, jnp.logical_not(odd))
    for j, copy in out_w.items():
        if j > DEEP:
            starts.setdefault((j, DEEP), []).append((has_outer, copy))
    rest = [out_w[j] for j in range(1, DEEP + 1)]
    for i, copy in enumerate(in_half):
        starts.setdefault((SWEEPS, layers - 1 - i), []).append((always, copy))

    def coefficients(u):
        for face in (u, u + 1):
            if face not in faces:
                bz[at(face)] = 0.5 * COUPLING * (k[at(face)] + k[at(face - 1)])
                faces.add(face)
        if u not in cells:
            coefficient_layer(k, bx, by, inv, at(u), COUPLING, keep_outer if u < 0 else 1.0)
            cells.add(u)

    def advance(values=(), conductivity=()):
        have.update(values)
        have_k.update(conductivity)
        for u in range(-DEEP, layers + SWEEPS - 1):
            if u not in cells and have_k >= {u - 1, u, u + 1}:
                coefficients(u)
        moved, leaving = True, []
        while moved:
            moved = False
            for j, u in list(waiting):
                first = SWEEPS * ((j - 1) // SWEEPS)
                inputs = {(j - 1, u - 1), (j - 1, u), (j - 1, u + 1), (first, u)}
                if u not in cells or not have >= inputs:
                    continue
                sweep_layer(
                    w[j - 1], w[first], w[j], bx, by, bz, inv, at(u),
                    weights[(j - 1) % SWEEPS],
                )
                have.add((j, u))
                del waiting[(j, u)]
                moved = True
                leaving += starts.get((j, u), [])
        for ok, copy in leaving:
            when(ok, copy.start)

    pl.semaphore_wait(barrier, expected)

    when(
        has_prev,
        lambda: pl.semaphore_signal(
            entered, inc=1, device_id=(cut - 1, gz), device_id_type=MESH
        ),
    )
    k_order = [*pieces_k[direct:], *pieces_k[:direct]]
    for copy in out_k[:1] + out_w0[:1]:
        when(early, copy.start)
    for u in k_order:
        when(carries if u >= direct else relays, out_k[u].start)
        if u == 0:
            when(relays, out_w0[0].start)
    for a, b in zip(in_k, in_w0):
        a.start()
        b.start()

    for load in loads_k + loads_s:
        load.wait()
    for i in range(HALO):
        if i == PACE:
            for copy in out_k[1:direct] + out_w0[1:]:
                when(early, copy.start)
        in_k[i].wait_recv()
        in_w0[i].wait_recv()
    advance([(0, u) for u in range(layers + HALO)], range(layers + HALO))

    near_c = range(coarse + HALO_C)

    @pl.when(has_prev)
    def _():
        both = restricted(
            [(ref, at(2 * c)) for ref in (k, w0) for c in near_c], tmp
        )
        for c in near_c:
            kc[HALO_C + c] = both[c]
            rs[HALO_C + c] = both[len(near_c) + c]
        shared[0] = both[HALO_C - 1]
        shared[1] = both[len(near_c) + HALO_C - 1]
        for i, u in enumerate(k_order):
            when(has_outer, out_k[u].wait_recv)
            if u >= direct:
                when(relays, relay_k[u - direct].start)
            if i == 0:
                for copy in out_w0[1:] + [out_w[j] for j in range(1, DEEP + 1)]:
                    when(relays, copy.start)
                when(has_outer, out_shared.start)

    first_waits = jnp.logical_and(has_outer, jnp.logical_not(has_prev))

    def arrival(what, index):
        if what == EDGES:
            for i in pieces_k:
                if pieces[i][0] == index:
                    when(first_waits, out_k[i].wait_recv)
            when(has_outer, out_w0[index].wait_recv)
            if index == 0:
                for copy in rest:
                    when(early, copy.start)
            return [(0, -1 - index)], [-1 - index]
        if what == HALF:
            for copy in in_half:
                copy.wait_recv()
            return [(SWEEPS, layers + i) for i in range(SWEEPS)], []
        when(has_outer, out_w[index].wait_recv)
        return [(index, -EDGE)], []

    for group in GROUPS:
        arrived = [arrival(*one) for one in group]
        advance(sum((v for v, _ in arrived), []), sum((c for _, c in arrived), []))

    @pl.when(has_next)
    def _():
        for c, value in enumerate(
            restricted([(w6, at(2 * c)) for c in range(coarse)], tmp)
        ):
            outgoing[c] = value

    @pl.when(has_prev)
    def _():
        kc[HALO_C - 1], rs[HALO_C - 1] = restricted(
            [(ref, at(-2)) for ref in (k, w0)], tmp
        )
        when(has_outer, out_shared.wait_recv)
        kc[0], rs[0] = given[0], given[1]
        for c in range(-1, coarse + 2):
            cz[HALO_C + c] = 0.25 * COUPLING * (kc[HALO_C + c] + kc[HALO_C + c - 1])
        for c in range(-1, coarse + 1):
            coefficient_layer(
                kc, cx, cy, cinv, HALO_C + c, 0.5 * COUPLING, keep_outer if c < 0 else 1.0
            )
        next_own.wait_recv()
        when(has_outer, next_out.wait_recv)
        next_in.wait_recv()
        for c in range(coarse):
            car[HALO_C + c] = car_own[c] - rs[HALO_C + c]
        for c in range(HALO_C):
            low, high = HALO_C - 1 - c, HALO_C + coarse + c
            car[low] = car_out[c] - rs[low]
            car[high] = car_in[HALO_C - 1 - c] - rs[high]
        steps = (car, ca, cb)
        for j, weight in enumerate(coarse_weights):
            beside = SWEEPS_C - 1 - j
            for c in range(-beside, coarse + beside):
                sweep_layer(
                    steps[j], car, steps[j + 1], cx, cy, cz, cinv, HALO_C + c, weight
                )

        @pl.when(has_next)
        def _():
            for c in range(coarse):
                outgoing[c] = outgoing[c] + cb[HALO_C + c]

    @pl.when(has_next)
    def _():
        pl.semaphore_wait(entered, 1)
        when(has_outer, next_out.start)
        next_in.start()
        next_own.start()

    @pl.when(has_prev)
    def _():
        rows = tmp.shape[1]
        for c in range(coarse):
            for parity in range(2):
                tmp[c, pl.ds(parity, rows // 2, 2), :] = cb[HALO_C + c]
        half = tmp.shape[2] // 2
        lane = lax.broadcasted_iota(jnp.int32, tmp.shape[1:], 1) // 2
        wide = jnp.concatenate(
            [
                jnp.concatenate([lanes(tmp[c], lane), lanes(tmp[c], lane + half)], axis=1)
                for c in range(coarse)
            ],
            axis=0,
        )
        for u in range(layers):
            out[0, place(u)] = w6[at(u)] + wide[(u // 2) * rows : (u // 2 + 1) * rows]

    @pl.when(jnp.logical_not(has_prev))
    def _():
        for u in range(layers):
            out[0, place(u)] = w6[at(u)]

    for ok, copy in sent:
        when(ok, copy.wait_send)


def shards(states, conduct):
    cut_count, gz_count = lax.axis_size("cuts"), lax.axis_size("gz")
    layers, nx, ny = conduct.shape
    assert gz_count % 2 == 0 and layers % 2 == 0 and layers >= HALO
    fine = pltpu.VMEM((layers + 2 * HALO, nx, ny), jnp.float32)

    def small(count):
        return pltpu.VMEM((count, nx // 2, ny // 2), jnp.float32)

    copies = 2 * HALO + 3 * EDGE + 1 + ROUNDS - DEEP - 1 + SWEEPS + 4
    return pl.pallas_call(
        functools.partial(kernel, cut_count, gz_count, layers),
        out_shape=pltpu.VMEM(states.shape, jnp.float32),
        in_specs=[pl.BlockSpec(memory_space=pl.ANY)] * 2,
        out_specs=pl.BlockSpec(memory_space=pltpu.VMEM),
        scratch_shapes=[fine] * 12
        + [pltpu.VMEM((layers + 2 * HALO_C, nx, ny // 2), jnp.float32)]
        + [small(layers // 2 + 2 * HALO_C)] * 9
        + [small(2), small(2)]
        + [small(layers // 2), small(HALO_C), small(HALO_C), small(layers // 2)]
        + [
            pltpu.SemaphoreType.DMA((2 * layers,)),
            pltpu.SemaphoreType.DMA((copies,)),
            pltpu.SemaphoreType.DMA((copies,)),
            pltpu.SemaphoreType.REGULAR,
        ],
        compiler_params=pltpu.CompilerParams(collective_id=0, has_side_effects=True),
        name="parareal",
    )(states, conduct)


def solution(mesh):
    in_specs = (P("cuts", "gz", None, None), P("gz", None, None))
    out_specs = P("cuts", "gz", None, None)
    return jax.shard_map(shards, mesh=mesh, in_specs=in_specs, out_specs=out_specs, check_vma=False)
```

```python
import functools
import math

import jax
import jax.numpy as jnp
from jax import lax
from jax.experimental import pallas as pl
from jax.experimental.pallas import tpu as pltpu
from jax.sharding import PartitionSpec as P

STEPS = 2
SWEEPS = 3
SWEEPS_C = 2

COUPLING = 1.0
SPREAD = 0.85
MESH = pl.DeviceIdType.MESH

HALO = 4
HALO_C = HALO // 2
ROUNDS = STEPS * SWEEPS
DEEP = ROUNDS // 2 - 1
EDGE = DEEP + 1
DIRECT = 2
PACE = 2
EDGES, HALF, DEEPER = "edge", "half", "deep"
GROUPS = (
    ((EDGES, 0),),
    ((EDGES, 1),),
    ((HALF, None),),
    ((EDGES, 2), (DEEPER, 1), (DEEPER, 2)),
    ((DEEPER, 3),),
)


def chebyshev_weights(count):
    return [
        1.0 / (1.0 + SPREAD * math.cos(math.pi * (2 * index_now + 1) / (2 * count)))
        for index_now in range(count)
    ]


def down(v, axis):
    return pltpu.roll(v, 1, axis)


def up(v, axis):
    return pltpu.roll(v, v.shape[axis] - 1, axis)


def coefficient_layer(k_ref, bx, by, inv, l, coupling, keep):
    shape = k_ref.shape[1:]
    at_x = lax.broadcasted_iota(jnp.int32, shape, 0)
    at_y = lax.broadcasted_iota(jnp.int32, shape, 1)
    half = 0.5 * coupling
    k = k_ref[l]
    x_lo = jnp.where(at_x == 0, 0.0, down(k, 0))
    x_hi = jnp.where(at_x == shape[0] - 1, 0.0, up(k, 0))
    y_lo = jnp.where(at_y == 0, 0.0, down(k, 1))
    y_hi = jnp.where(at_y == shape[1] - 1, 0.0, up(k, 1))
    bx[l] = jnp.where(at_x == 0, 0.0, half * (k + x_lo))
    by[l] = jnp.where(at_y == 0, 0.0, half * (k + y_lo))
    diag = 1.0 + half * (
        6.0 * k + (x_lo + x_hi) + (y_lo + y_hi) + (k_ref[l - 1] + k_ref[l + 1])
    )
    inv[l] = keep / diag


def sweep_layer(src, source, dst, bx, by, bz, inv, l, weight):
    w = src[l]
    b_y = by[l]
    b_x = bx[l]
    total = (
        source[l]
        + (b_y * down(w, 1) + up(b_y * w, 1))
        + (b_x * down(w, 0) + up(b_x * w, 0))
        + (bz[l] * src[l - 1] + bz[l + 1] * src[l + 1])
    )
    dst[l] = (1.0 - weight) * w + (weight * inv[l]) * total


def lanes(v, index):
    return jnp.take_along_axis(v, index, axis=1)


def restricted(pairs, tmp):
    rows = tmp.shape[1]
    width = tmp.shape[2]
    lane = lax.broadcasted_iota(jnp.int32, (rows, width), 1)
    even = lax.rem(2 * lane, width)
    out = []
    for j, (field, first) in enumerate(pairs):
        v = field[first] + field[first + 1]
        v = 0.125 * (v + up(v, 1))
        tmp[j] = jnp.where(lane < width // 2, lanes(v[:, :width], even), lanes(v[:, width:], even))
        out.append(tmp[j, pl.ds(0, rows // 2, 2), :] + tmp[j, pl.ds(1, rows // 2, 2), :])
    return out


def kernel(
    cut_count, gz_count, layers,
    s_in, k_in, out,
    k, w0, w1, w2, w3, w4, w5, w6, bx, by, bz, inv, tmp,
    kc, cx, cy, cz, cinv, rs, car, ca, cb, shared, given, car_own, car_out, car_in, outgoing,
    load_sem, send_sem, recv_sem, entered,
):
    cut = lax.axis_index("cuts")
    gz = lax.axis_index("gz")
    side = lax.rem(gz, 2)
    outer, inner = gz - 1 + 2 * side, gz + 1 - 2 * side
    has_outer = jnp.logical_and(outer >= 0, outer < gz_count)
    has_prev, has_next = cut > 0, cut < cut_count - 1
    odd = lax.rem(cut, 2) == 1
    relayed = jnp.logical_and(jnp.logical_not(odd), has_next)
    coarse = layers // 2
    always = None
    w = (w0, w1, w2, w3, w4, w5, w6)

    def at(u):
        return HALO + u

    def place(u):
        return u + side * (layers - 1 - 2 * u)

    def when(condition, act):
        if condition is always:
            act()
        else:
            pl.when(condition)(act)

    loads_k = [
        pltpu.make_async_copy(k_in.at[place(u)], k.at[at(u)], load_sem.at[u])
        for u in range(layers)
    ]
    loads_s = [
        pltpu.make_async_copy(s_in.at[0, place(u)], w0.at[at(u)], load_sem.at[layers + u])
        for u in range(layers)
    ]
    for load in loads_k + loads_s:
        load.start()

    barrier = pltpu.get_barrier_semaphore()
    for there, ok in (
        ((cut, outer), has_outer),
        ((cut, inner), always),
        ((cut + 1, gz), has_next),
    ):
        when(
            ok,
            lambda there=there: pl.semaphore_signal(
                barrier, inc=1, device_id=there, device_id_type=MESH
            ),
        )
    expected = 1 + has_outer.astype(jnp.int32) + has_prev.astype(jnp.int32)

    @pl.when(jnp.logical_not(has_outer))
    def _():
        fine = jnp.zeros((EDGE,) + w0.shape[1:], jnp.float32)
        for ref in (w0, k):
            ref[pl.ds(at(-EDGE), EDGE)] = fine
        for j in range(1, ROUNDS - DEEP):
            w[j][at(-EDGE)] = fine[0]
        given[...] = jnp.zeros(given.shape, jnp.float32)
        car_out[...] = jnp.zeros(car_out.shape, jnp.float32)

    count = [0]
    sent = []

    def remote(src, dst, there, ok, slot=None):
        index = count[0]
        count[0] += 1
        copy = pltpu.make_async_remote_copy(
            src_ref=src,
            dst_ref=dst,
            send_sem=send_sem.at[index],
            recv_sem=recv_sem.at[index if slot is None else slot],
            device_id=there,
            device_id_type=MESH,
        )
        sent.append((ok, copy))
        return copy

    to_outer, to_inner = (cut, outer), (cut, inner)
    carries = jnp.logical_and(has_outer, jnp.logical_not(relayed))
    relays = jnp.logical_and(has_outer, odd)

    def own_k(u):
        return k_in.at[place(u)]

    def own_s(u):
        return s_in.at[0, place(u)]

    def mirrored(src, ref, u, ok):
        return remote(src, ref.at[at(-1 - u)], to_outer, ok)

    out_k = [
        mirrored(own_k(u), k, u, has_outer if u < DIRECT else carries) for u in range(EDGE)
    ]
    out_w0 = [mirrored(own_s(u), w0, u, has_outer) for u in range(EDGE)]
    out_w = {
        j: mirrored(w[j].at[at(DEEP)], w[j], DEEP, has_outer)
        for j in range(1, ROUNDS - DEEP)
    }
    relay_k = [
        remote(k.at[at(-1 - u)], k.at[at(-1 - u)], (cut - 1, gz), relays, slot=u)
        for u in range(DIRECT, EDGE)
    ]

    def across(src, ref, i):
        return remote(src, ref.at[at(layers + i)], to_inner, always)

    in_k = [across(own_k(layers - 1 - i), k, i) for i in range(HALO)]
    in_w0 = [across(own_s(layers - 1 - i), w0, i) for i in range(HALO)]
    in_half = [
        across(w[SWEEPS].at[at(layers - 1 - i)], w[SWEEPS], i) for i in range(SWEEPS)
    ]
    out_shared = remote(
        shared, given, to_outer, jnp.logical_and(has_prev, has_outer)
    )
    next_own = remote(outgoing, car_own, (cut + 1, gz), has_next)
    next_out = remote(
        outgoing.at[pl.ds(0, HALO_C)], car_out, (cut + 1, outer),
        jnp.logical_and(has_next, has_outer),
    )
    next_in = remote(
        outgoing.at[pl.ds(coarse - HALO_C, HALO_C)], car_in, (cut + 1, inner), has_next
    )

    keep_outer = jnp.where(has_outer, 1.0, 0.0)
    weights = chebyshev_weights(SWEEPS)
    coarse_weights = chebyshev_weights(SWEEPS_C)

    needed = []
    for j in range(1, ROUNDS + 1):
        low = -min(DEEP, ROUNDS - j)
        high = layers + (-j % SWEEPS)
        needed += [(j, u) for u in range(low, high)]
    waiting = dict.fromkeys(needed)
    have, have_k, faces, cells = set(), set(), set(), set()
    starts = {}
    early = jnp.logical_and(has_outer, jnp.logical_not(odd))
    for j, copy in out_w.items():
        if j > DEEP:
            starts.setdefault((j, DEEP), []).append((has_outer, copy))
    rest = [out_w[j] for j in range(1, DEEP + 1)]
    for i, copy in enumerate(in_half):
        starts.setdefault((SWEEPS, layers - 1 - i), []).append((always, copy))

    def coefficients(u):
        for face in (u, u + 1):
            if face not in faces:
                bz[at(face)] = 0.5 * COUPLING * (k[at(face)] + k[at(face - 1)])
                faces.add(face)
        if u not in cells:
            coefficient_layer(k, bx, by, inv, at(u), COUPLING, keep_outer if u < 0 else 1.0)
            cells.add(u)

    def advance(values=(), conductivity=()):
        have.update(values)
        have_k.update(conductivity)
        for u in range(-DEEP, layers + SWEEPS - 1):
            if u not in cells and have_k >= {u - 1, u, u + 1}:
                coefficients(u)
        moved, leaving = True, []
        while moved:
            moved = False
            for j, u in list(waiting):
                first = SWEEPS * ((j - 1) // SWEEPS)
                inputs = {(j - 1, u - 1), (j - 1, u), (j - 1, u + 1), (first, u)}
                if u not in cells or not have >= inputs:
                    continue
                sweep_layer(
                    w[j - 1], w[first], w[j], bx, by, bz, inv, at(u),
                    weights[(j - 1) % SWEEPS],
                )
                have.add((j, u))
                del waiting[(j, u)]
                moved = True
                leaving += starts.get((j, u), [])
        for ok, copy in leaving:
            when(ok, copy.start)

    pl.semaphore_wait(barrier, expected)

    when(
        has_prev,
        lambda: pl.semaphore_signal(
            entered, inc=1, device_id=(cut - 1, gz), device_id_type=MESH
        ),
    )
    k_order = [*range(DIRECT, EDGE), *range(DIRECT)]
    for copy in out_k[:1] + out_w0[:1]:
        when(early, copy.start)
    for u in k_order:
        when(carries if u >= DIRECT else relays, out_k[u].start)
        if u == 0:
            when(relays, out_w0[0].start)
    for a, b in zip(in_k, in_w0):
        a.start()
        b.start()

    for load in loads_k + loads_s:
        load.wait()
    for i in range(HALO):
        if i == PACE:
            for copy in out_k[1:DIRECT] + out_w0[1:]:
                when(early, copy.start)
        in_k[i].wait_recv()
        in_w0[i].wait_recv()
    advance([(0, u) for u in range(layers + HALO)], range(layers + HALO))

    near_c = range(coarse + HALO_C)

    @pl.when(has_prev)
    def _():
        both = restricted(
            [(ref, at(2 * c)) for ref in (k, w0) for c in near_c], tmp
        )
        for c in near_c:
            kc[HALO_C + c] = both[c]
            rs[HALO_C + c] = both[len(near_c) + c]
        shared[0] = both[HALO_C - 1]
        shared[1] = both[len(near_c) + HALO_C - 1]
        for i, u in enumerate(k_order):
            when(has_outer, out_k[u].wait_recv)
            if u >= DIRECT:
                when(relays, relay_k[u - DIRECT].start)
            if i == 0:
                for copy in out_w0[1:] + rest:
                    when(relays, copy.start)
                when(has_outer, out_shared.start)

    first_waits = jnp.logical_and(has_outer, jnp.logical_not(has_prev))

    def arrival(what, index):
        if what == EDGES:
            when(first_waits, out_k[index].wait_recv)
            when(has_outer, out_w0[index].wait_recv)
            if index == 0:
                for copy in rest:
                    when(early, copy.start)
            return [(0, -1 - index)], [-1 - index]
        if what == HALF:
            for copy in in_half:
                copy.wait_recv()
            return [(SWEEPS, layers + i) for i in range(SWEEPS)], []
        when(has_outer, out_w[index].wait_recv)
        return [(index, -EDGE)], []

    for group in GROUPS:
        arrived = [arrival(*one) for one in group]
        advance(sum((v for v, _ in arrived), []), sum((c for _, c in arrived), []))

    @pl.when(has_next)
    def _():
        for c, value in enumerate(
            restricted([(w6, at(2 * c)) for c in range(coarse)], tmp)
        ):
            outgoing[c] = value

    @pl.when(has_prev)
    def _():
        kc[HALO_C - 1], rs[HALO_C - 1] = restricted(
            [(ref, at(-2)) for ref in (k, w0)], tmp
        )
        when(has_outer, out_shared.wait_recv)
        kc[0], rs[0] = given[0], given[1]
        for c in range(-1, coarse + 2):
            cz[HALO_C + c] = 0.25 * COUPLING * (kc[HALO_C + c] + kc[HALO_C + c - 1])
        for c in range(-1, coarse + 1):
            coefficient_layer(
                kc, cx, cy, cinv, HALO_C + c, 0.5 * COUPLING, keep_outer if c < 0 else 1.0
            )
        next_own.wait_recv()
        when(has_outer, next_out.wait_recv)
        next_in.wait_recv()
        for c in range(coarse):
            car[HALO_C + c] = car_own[c] - rs[HALO_C + c]
        for c in range(HALO_C):
            low, high = HALO_C - 1 - c, HALO_C + coarse + c
            car[low] = car_out[c] - rs[low]
            car[high] = car_in[HALO_C - 1 - c] - rs[high]
        steps = (car, ca, cb)
        for j, weight in enumerate(coarse_weights):
            beside = SWEEPS_C - 1 - j
            for c in range(-beside, coarse + beside):
                sweep_layer(
                    steps[j], car, steps[j + 1], cx, cy, cz, cinv, HALO_C + c, weight
                )

        @pl.when(has_next)
        def _():
            for c in range(coarse):
                outgoing[c] = outgoing[c] + cb[HALO_C + c]

    @pl.when(has_next)
    def _():
        pl.semaphore_wait(entered, 1)
        when(has_outer, next_out.start)
        next_in.start()
        next_own.start()

    @pl.when(has_prev)
    def _():
        rows = tmp.shape[1]
        for c in range(coarse):
            for parity in range(2):
                tmp[c, pl.ds(parity, rows // 2, 2), :] = cb[HALO_C + c]
        half = tmp.shape[2] // 2
        lane = lax.broadcasted_iota(jnp.int32, tmp.shape[1:], 1) // 2
        wide = jnp.concatenate(
            [
                jnp.concatenate([lanes(tmp[c], lane), lanes(tmp[c], lane + half)], axis=1)
                for c in range(coarse)
            ],
            axis=0,
        )
        for u in range(layers):
            out[0, place(u)] = w6[at(u)] + wide[(u // 2) * rows : (u // 2 + 1) * rows]

    @pl.when(jnp.logical_not(has_prev))
    def _():
        for u in range(layers):
            out[0, place(u)] = w6[at(u)]

    for ok, copy in sent:
        when(ok, copy.wait_send)


def shards(states, conduct):
    cut_count, gz_count = lax.axis_size("cuts"), lax.axis_size("gz")
    layers, nx, ny = conduct.shape
    assert gz_count % 2 == 0 and layers % 2 == 0 and layers >= HALO
    fine = pltpu.VMEM((layers + 2 * HALO, nx, ny), jnp.float32)

    def small(count):
        return pltpu.VMEM((count, nx // 2, ny // 2), jnp.float32)

    copies = 2 * HALO + 3 * EDGE - DIRECT + ROUNDS - DEEP - 1 + SWEEPS + 4
    return pl.pallas_call(
        functools.partial(kernel, cut_count, gz_count, layers),
        out_shape=pltpu.VMEM(states.shape, jnp.float32),
        in_specs=[pl.BlockSpec(memory_space=pl.ANY)] * 2,
        out_specs=pl.BlockSpec(memory_space=pltpu.VMEM),
        scratch_shapes=[fine] * 12
        + [pltpu.VMEM((layers + 2 * HALO_C, nx, ny // 2), jnp.float32)]
        + [small(layers // 2 + 2 * HALO_C)] * 9
        + [small(2), small(2)]
        + [small(layers // 2), small(HALO_C), small(HALO_C), small(layers // 2)]
        + [
            pltpu.SemaphoreType.DMA((2 * layers,)),
            pltpu.SemaphoreType.DMA((copies,)),
            pltpu.SemaphoreType.DMA((copies,)),
            pltpu.SemaphoreType.REGULAR,
        ],
        compiler_params=pltpu.CompilerParams(collective_id=0, has_side_effects=True),
        name="parareal",
    )(states, conduct)


def solution(mesh):
    in_specs = (P("cuts", "gz", None, None), P("gz", None, None))
    out_specs = P("cuts", "gz", None, None)
    return jax.shard_map(shards, mesh=mesh, in_specs=in_specs, out_specs=out_specs, check_vma=False)
```

```python
import functools
import math

import jax
import jax.numpy as jnp
from jax import lax
from jax.experimental import pallas as pl
from jax.experimental.pallas import tpu as pltpu
from jax.sharding import PartitionSpec as P

STEPS = 2
SWEEPS = 3
SWEEPS_C = 2

COUPLING = 1.0
SPREAD = 0.85
MESH = pl.DeviceIdType.MESH

HALO = 4
HALO_C = HALO // 2
ROUNDS = STEPS * SWEEPS
DEEP = ROUNDS // 2 - 1
EDGE = DEEP + 1
DIRECT = 2
PACE = 2
EDGES, HALF, DEEPER = "edge", "half", "deep"
GROUPS = (
    ((EDGES, 0),),
    ((EDGES, 1),),
    ((HALF, None),),
    ((EDGES, 2), (DEEPER, 1), (DEEPER, 2)),
    ((DEEPER, 3),),
)


def chebyshev_weights(count):
    return [
        1.0 / (1.0 + SPREAD * math.cos(math.pi * (2 * index_now + 1) / (2 * count)))
        for index_now in range(count)
    ]


def down(v, axis):
    return pltpu.roll(v, 1, axis)


def up(v, axis):
    return pltpu.roll(v, v.shape[axis] - 1, axis)


def coefficient_layer(k_ref, bx, by, inv, l, coupling, keep):
    shape = k_ref.shape[1:]
    at_x = lax.broadcasted_iota(jnp.int32, shape, 0)
    at_y = lax.broadcasted_iota(jnp.int32, shape, 1)
    half = 0.5 * coupling
    k = k_ref[l]
    x_lo = jnp.where(at_x == 0, 0.0, down(k, 0))
    x_hi = jnp.where(at_x == shape[0] - 1, 0.0, up(k, 0))
    y_lo = jnp.where(at_y == 0, 0.0, down(k, 1))
    y_hi = jnp.where(at_y == shape[1] - 1, 0.0, up(k, 1))
    bx[l] = jnp.where(at_x == 0, 0.0, half * (k + x_lo))
    by[l] = jnp.where(at_y == 0, 0.0, half * (k + y_lo))
    diag = 1.0 + half * (
        6.0 * k + (x_lo + x_hi) + (y_lo + y_hi) + (k_ref[l - 1] + k_ref[l + 1])
    )
    inv[l] = keep / diag


def sweep_layer(src, source, dst, bx, by, bz, inv, l, weight):
    w = src[l]
    b_y = by[l]
    b_x = bx[l]
    total = (
        source[l]
        + (b_y * down(w, 1) + up(b_y * w, 1))
        + (b_x * down(w, 0) + up(b_x * w, 0))
        + (bz[l] * src[l - 1] + bz[l + 1] * src[l + 1])
    )
    dst[l] = (1.0 - weight) * w + (weight * inv[l]) * total


def lanes(v, index):
    return jnp.take_along_axis(v, index, axis=1)


def restricted(pairs, tmp):
    rows = tmp.shape[1]
    width = tmp.shape[2]
    lane = lax.broadcasted_iota(jnp.int32, (rows, width), 1)
    even = lax.rem(2 * lane, width)
    out = []
    for j, (field, first) in enumerate(pairs):
        v = field[first] + field[first + 1]
        v = 0.125 * (v + up(v, 1))
        tmp[j] = jnp.where(lane < width // 2, lanes(v[:, :width], even), lanes(v[:, width:], even))
        out.append(tmp[j, pl.ds(0, rows // 2, 2), :] + tmp[j, pl.ds(1, rows // 2, 2), :])
    return out


def kernel(
    cut_count, gz_count, layers,
    s_in, k_in, out,
    k, w0, w1, w2, w3, w4, w5, w6, bx, by, bz, inv, tmp,
    kc, cx, cy, cz, cinv, rs, car, ca, cb, shared, given, car_own, car_out, car_in, outgoing,
    load_sem, send_sem, recv_sem, entered,
):
    cut = lax.axis_index("cuts")
    gz = lax.axis_index("gz")
    side = lax.rem(gz, 2)
    outer, inner = gz - 1 + 2 * side, gz + 1 - 2 * side
    has_outer = jnp.logical_and(outer >= 0, outer < gz_count)
    has_prev, has_next = cut > 0, cut < cut_count - 1
    odd = lax.rem(cut, 2) == 1
    relayed = jnp.logical_and(jnp.logical_not(odd), has_next)
    coarse = layers // 2
    always = None
    w = (w0, w1, w2, w3, w4, w5, w6)

    def at(u):
        return HALO + u

    def place(u):
        return u + side * (layers - 1 - 2 * u)

    def when(condition, act):
        if condition is always:
            act()
        else:
            pl.when(condition)(act)

    loads_k = [
        pltpu.make_async_copy(k_in.at[place(u)], k.at[at(u)], load_sem.at[u])
        for u in range(layers)
    ]
    loads_s = [
        pltpu.make_async_copy(s_in.at[0, place(u)], w0.at[at(u)], load_sem.at[layers + u])
        for u in range(layers)
    ]
    for load in loads_k + loads_s:
        load.start()

    barrier = pltpu.get_barrier_semaphore()
    for there, ok in (
        ((cut, outer), has_outer),
        ((cut, inner), always),
        ((cut + 1, gz), has_next),
    ):
        when(
            ok,
            lambda there=there: pl.semaphore_signal(
                barrier, inc=1, device_id=there, device_id_type=MESH
            ),
        )
    expected = 1 + has_outer.astype(jnp.int32) + has_prev.astype(jnp.int32)

    @pl.when(jnp.logical_not(has_outer))
    def _():
        fine = jnp.zeros((EDGE,) + w0.shape[1:], jnp.float32)
        for ref in (w0, k):
            ref[pl.ds(at(-EDGE), EDGE)] = fine
        for j in range(1, ROUNDS - DEEP):
            w[j][at(-EDGE)] = fine[0]
        given[...] = jnp.zeros(given.shape, jnp.float32)
        car_out[...] = jnp.zeros(car_out.shape, jnp.float32)

    count = [0]
    sent = []

    def remote(src, dst, there, ok, slot=None):
        index = count[0]
        count[0] += 1
        copy = pltpu.make_async_remote_copy(
            src_ref=src,
            dst_ref=dst,
            send_sem=send_sem.at[index],
            recv_sem=recv_sem.at[index if slot is None else slot],
            device_id=there,
            device_id_type=MESH,
        )
        sent.append((ok, copy))
        return copy

    to_outer, to_inner = (cut, outer), (cut, inner)
    carries = jnp.logical_and(has_outer, jnp.logical_not(relayed))
    relays = jnp.logical_and(has_outer, odd)

    def own_k(u):
        return k_in.at[place(u)]

    def own_s(u):
        return s_in.at[0, place(u)]

    def mirrored(src, ref, u, ok):
        return remote(src, ref.at[at(-1 - u)], to_outer, ok)

    out_k = [
        mirrored(own_k(u), k, u, has_outer if u < DIRECT else carries) for u in range(EDGE)
    ]
    out_w0 = [mirrored(own_s(u), w0, u, has_outer) for u in range(EDGE)]
    out_w = {
        j: mirrored(w[j].at[at(DEEP)], w[j], DEEP, has_outer)
        for j in range(1, ROUNDS - DEEP)
    }
    relay_k = [
        remote(k.at[at(-1 - u)], k.at[at(-1 - u)], (cut - 1, gz), relays, slot=u)
        for u in range(DIRECT, EDGE)
    ]

    def across(src, ref, i):
        return remote(src, ref.at[at(layers + i)], to_inner, always)

    in_k = [across(own_k(layers - 1 - i), k, i) for i in range(HALO)]
    in_w0 = [across(own_s(layers - 1 - i), w0, i) for i in range(HALO)]
    in_half = [
        across(w[SWEEPS].at[at(layers - 1 - i)], w[SWEEPS], i) for i in range(SWEEPS)
    ]
    out_shared = remote(
        shared, given, to_outer, jnp.logical_and(has_prev, has_outer)
    )
    next_own = remote(outgoing, car_own, (cut + 1, gz), has_next)
    next_out = remote(
        outgoing.at[pl.ds(0, HALO_C)], car_out, (cut + 1, outer),
        jnp.logical_and(has_next, has_outer),
    )
    next_in = remote(
        outgoing.at[pl.ds(coarse - HALO_C, HALO_C)], car_in, (cut + 1, inner), has_next
    )

    keep_outer = jnp.where(has_outer, 1.0, 0.0)
    weights = chebyshev_weights(SWEEPS)
    coarse_weights = chebyshev_weights(SWEEPS_C)

    needed = []
    for j in range(1, ROUNDS + 1):
        low = -min(DEEP, ROUNDS - j)
        high = layers + (-j % SWEEPS)
        needed += [(j, u) for u in range(low, high)]
    waiting = dict.fromkeys(needed)
    have, have_k, faces, cells = set(), set(), set(), set()
    starts = {}
    early = jnp.logical_and(has_outer, jnp.logical_not(odd))
    for j, copy in out_w.items():
        if j > DEEP:
            starts.setdefault((j, DEEP), []).append((has_outer, copy))
    rest = [out_w[j] for j in range(1, DEEP + 1)]
    for i, copy in enumerate(in_half):
        starts.setdefault((SWEEPS, layers - 1 - i), []).append((always, copy))

    def coefficients(u):
        for face in (u, u + 1):
            if face not in faces:
                bz[at(face)] = 0.5 * COUPLING * (k[at(face)] + k[at(face - 1)])
                faces.add(face)
        if u not in cells:
            coefficient_layer(k, bx, by, inv, at(u), COUPLING, keep_outer if u < 0 else 1.0)
            cells.add(u)

    def advance(values=(), conductivity=()):
        have.update(values)
        have_k.update(conductivity)
        for u in range(-DEEP, layers + SWEEPS - 1):
            if u not in cells and have_k >= {u - 1, u, u + 1}:
                coefficients(u)
        moved, leaving = True, []
        while moved:
            moved = False
            for j, u in list(waiting):
                first = SWEEPS * ((j - 1) // SWEEPS)
                inputs = {(j - 1, u - 1), (j - 1, u), (j - 1, u + 1), (first, u)}
                if u not in cells or not have >= inputs:
                    continue
                sweep_layer(
                    w[j - 1], w[first], w[j], bx, by, bz, inv, at(u),
                    weights[(j - 1) % SWEEPS],
                )
                have.add((j, u))
                del waiting[(j, u)]
                moved = True
                leaving += starts.get((j, u), [])
        for ok, copy in leaving:
            when(ok, copy.start)

    pl.semaphore_wait(barrier, expected)

    when(
        has_prev,
        lambda: pl.semaphore_signal(
            entered, inc=1, device_id=(cut - 1, gz), device_id_type=MESH
        ),
    )
    k_order = [*range(DIRECT, EDGE), *range(DIRECT)]
    for copy in out_k[:1] + out_w0[:1] + out_k[1:DIRECT]:
        when(early, copy.start)
    for u in k_order:
        when(carries if u >= DIRECT else relays, out_k[u].start)
        if u == 0:
            when(relays, out_w0[0].start)
    for a, b in zip(in_k, in_w0):
        a.start()
        b.start()

    for load in loads_k + loads_s:
        load.wait()
    for i in range(HALO):
        if i == PACE:
            for copy in out_w0[1:]:
                when(early, copy.start)
        in_k[i].wait_recv()
        in_w0[i].wait_recv()
    advance([(0, u) for u in range(layers + HALO)], range(layers + HALO))

    near_c = range(coarse + HALO_C)

    @pl.when(has_prev)
    def _():
        both = restricted(
            [(ref, at(2 * c)) for ref in (k, w0) for c in near_c], tmp
        )
        for c in near_c:
            kc[HALO_C + c] = both[c]
            rs[HALO_C + c] = both[len(near_c) + c]
        shared[0] = both[HALO_C - 1]
        shared[1] = both[len(near_c) + HALO_C - 1]
        for i, u in enumerate(k_order):
            when(has_outer, out_k[u].wait_recv)
            if u >= DIRECT:
                when(relays, relay_k[u - DIRECT].start)
            if i == 0:
                for copy in out_w0[1:] + rest:
                    when(relays, copy.start)
                when(has_outer, out_shared.start)

    first_waits = jnp.logical_and(has_outer, jnp.logical_not(has_prev))

    def arrival(what, index):
        if what == EDGES:
            when(first_waits, out_k[index].wait_recv)
            when(has_outer, out_w0[index].wait_recv)
            if index == 0:
                for copy in rest:
                    when(early, copy.start)
            return [(0, -1 - index)], [-1 - index]
        if what == HALF:
            for copy in in_half:
                copy.wait_recv()
            return [(SWEEPS, layers + i) for i in range(SWEEPS)], []
        when(has_outer, out_w[index].wait_recv)
        return [(index, -EDGE)], []

    for group in GROUPS:
        arrived = [arrival(*one) for one in group]
        advance(sum((v for v, _ in arrived), []), sum((c for _, c in arrived), []))

    @pl.when(has_next)
    def _():
        for c, value in enumerate(
            restricted([(w6, at(2 * c)) for c in range(coarse)], tmp)
        ):
            outgoing[c] = value

    @pl.when(has_prev)
    def _():
        kc[HALO_C - 1], rs[HALO_C - 1] = restricted(
            [(ref, at(-2)) for ref in (k, w0)], tmp
        )
        when(has_outer, out_shared.wait_recv)
        kc[0], rs[0] = given[0], given[1]
        for c in range(-1, coarse + 2):
            cz[HALO_C + c] = 0.25 * COUPLING * (kc[HALO_C + c] + kc[HALO_C + c - 1])
        for c in range(-1, coarse + 1):
            coefficient_layer(
                kc, cx, cy, cinv, HALO_C + c, 0.5 * COUPLING, keep_outer if c < 0 else 1.0
            )
        next_own.wait_recv()
        when(has_outer, next_out.wait_recv)
        next_in.wait_recv()
        for c in range(coarse):
            car[HALO_C + c] = car_own[c] - rs[HALO_C + c]
        for c in range(HALO_C):
            low, high = HALO_C - 1 - c, HALO_C + coarse + c
            car[low] = car_out[c] - rs[low]
            car[high] = car_in[HALO_C - 1 - c] - rs[high]
        steps = (car, ca, cb)
        for j, weight in enumerate(coarse_weights):
            beside = SWEEPS_C - 1 - j
            for c in range(-beside, coarse + beside):
                sweep_layer(
                    steps[j], car, steps[j + 1], cx, cy, cz, cinv, HALO_C + c, weight
                )

        @pl.when(has_next)
        def _():
            for c in range(coarse):
                outgoing[c] = outgoing[c] + cb[HALO_C + c]

    @pl.when(has_next)
    def _():
        pl.semaphore_wait(entered, 1)
        when(has_outer, next_out.start)
        next_in.start()
        next_own.start()

    @pl.when(has_prev)
    def _():
        rows = tmp.shape[1]
        for c in range(coarse):
            for parity in range(2):
                tmp[c, pl.ds(parity, rows // 2, 2), :] = cb[HALO_C + c]
        half = tmp.shape[2] // 2
        lane = lax.broadcasted_iota(jnp.int32, tmp.shape[1:], 1) // 2
        wide = jnp.concatenate(
            [
                jnp.concatenate([lanes(tmp[c], lane), lanes(tmp[c], lane + half)], axis=1)
                for c in range(coarse)
            ],
            axis=0,
        )
        for u in range(layers):
            out[0, place(u)] = w6[at(u)] + wide[(u // 2) * rows : (u // 2 + 1) * rows]

    @pl.when(jnp.logical_not(has_prev))
    def _():
        for u in range(layers):
            out[0, place(u)] = w6[at(u)]

    for ok, copy in sent:
        when(ok, copy.wait_send)


def shards(states, conduct):
    cut_count, gz_count = lax.axis_size("cuts"), lax.axis_size("gz")
    layers, nx, ny = conduct.shape
    assert gz_count % 2 == 0 and layers % 2 == 0 and layers >= HALO
    fine = pltpu.VMEM((layers + 2 * HALO, nx, ny), jnp.float32)

    def small(count):
        return pltpu.VMEM((count, nx // 2, ny // 2), jnp.float32)

    copies = 2 * HALO + 3 * EDGE - DIRECT + ROUNDS - DEEP - 1 + SWEEPS + 4
    return pl.pallas_call(
        functools.partial(kernel, cut_count, gz_count, layers),
        out_shape=pltpu.VMEM(states.shape, jnp.float32),
        in_specs=[pl.BlockSpec(memory_space=pl.ANY)] * 2,
        out_specs=pl.BlockSpec(memory_space=pltpu.VMEM),
        scratch_shapes=[fine] * 12
        + [pltpu.VMEM((layers + 2 * HALO_C, nx, ny // 2), jnp.float32)]
        + [small(layers // 2 + 2 * HALO_C)] * 9
        + [small(2), small(2)]
        + [small(layers // 2), small(HALO_C), small(HALO_C), small(layers // 2)]
        + [
            pltpu.SemaphoreType.DMA((2 * layers,)),
            pltpu.SemaphoreType.DMA((copies,)),
            pltpu.SemaphoreType.DMA((copies,)),
            pltpu.SemaphoreType.REGULAR,
        ],
        compiler_params=pltpu.CompilerParams(collective_id=0, has_side_effects=True),
        name="parareal",
    )(states, conduct)


def solution(mesh):
    in_specs = (P("cuts", "gz", None, None), P("gz", None, None))
    out_specs = P("cuts", "gz", None, None)
    return jax.shard_map(shards, mesh=mesh, in_specs=in_specs, out_specs=out_specs, check_vma=False)
```
